128 devices in a mesh: planes: 16 (over y, x_lo, core), rows: 8 (over x_hi, z).
Axes of the slice: x: 4 (x_hi: 2, x_lo: 2; x = x_hi * 2 + x_lo), y: 4, z: 4, core: 2. Of those that a mesh axis runs over, the one named last changes fastest.
Arguments:
- observed: float32 [16, 1024, 1024], P('planes', 'rows'), may hold values from -6 to 6
- estimate: float32 [16, 1024, 1024], P('planes', 'rows'), may hold values from -6 to 6
- spectrum: float32 [16, 1024, 1024], P('planes', 'rows'), may hold values from 0.1 to 1
Outputs:
- restored: float32 [16, 1024, 1024], P('planes', 'rows')
- residual: float32 [16, 1024, 1024], P('planes', 'rows')
The draws below stay inside these ranges and needn't reach their ends.
All inputs are finite; a program needn't handle non-finite values.
Results may differ from the reference program's by a relative error of at most 0.00014.
Values sent between devices are 32-bit elements; how exact they have to be, the bound alone decides.
No kernel may reach another device: no remote copies, remote signals or barrier semaphores. Data moves between devices by JAX's collectives and lax.ppermute only.
A program may use at most 128 MiB of HBM per device.

```python
import math
import jax
import jax.numpy as jnp
from jax import lax

N = 1024
SWEEPS = 1
ITERS = 1
PLANES = 16


def level_of(rng, shape, split, smallest, top_value):
    gain, own = 1.0, jax.random.fold_in(rng, 6)
    for dim, parts in split:
        draws = jnp.exp(jax.random.uniform(jax.random.fold_in(own, dim), (parts,), jnp.float32, smallest / len(split), top_value / len(split)))
        gain = gain * jnp.repeat(draws, shape[dim] // parts).reshape([-1 if axis == dim else 1 for axis in range(len(shape))])
    return gain


def noise(rng, shape, spread, most, cuts=(), kind=jnp.bfloat16):
    factor_of = level_of(rng, shape, cuts, -0.22, 0.18) if cuts else 1.0
    values = jax.random.normal(rng, shape, jnp.float32) * spread * factor_of
    return jnp.minimum(jnp.maximum(values, -most), most).astype(kind)


def setup_inputs(seed: int = 0) -> dict:
    keys = jax.random.split(jax.random.key(seed), 4)
    observed = noise(keys[0], (PLANES, N, N), 1.0, 6.0, ((0, 16), (1, 8)), jnp.float32)
    estimate = noise(keys[1], (PLANES, N, N), 1.0, 6.0, ((0, 16), (1, 8)), jnp.float32)
    spectrum = jnp.clip(jnp.exp(math.log(1.0) - 2.3025851 * jax.random.uniform(keys[2], (PLANES, N, N), jnp.float32) ** level_of(keys[2], (PLANES, N, N), ((0, 16), (1, 8)), -0.2, 0.2)), 0.1, 1.0)
    return dict(observed=observed, estimate=estimate, spectrum=spectrum)


HUBER_EDGE = 0.5
SMOOTHING = 0.3
PRECISE = lax.Precision.HIGHEST

def cosine_block(freq_start, freq_length, sample_start, sample_length, extent):
    frequency = freq_start + lax.iota(jnp.int32, freq_length)[:, None]
    sample = sample_start + lax.iota(jnp.int32, sample_length)[None, :]
    residue = (2 * sample + 1) * frequency % (4 * extent)
    angles = residue.astype(jnp.float32) * (math.pi / (2.0 * extent))
    norming = jnp.where(frequency == 0, math.sqrt(1.0 / extent), math.sqrt(2.0 / extent)).astype(jnp.float32)
    return jnp.cos(angles) * norming

def forward(source, cosines):
    spectral = jnp.einsum('kj,pjl->pkl', cosines, source, precision=PRECISE)
    return jnp.einsum('pkj,lj->pkl', spectral, cosines, precision=PRECISE)

def inverse(spectral, cosines):
    row_pass = jnp.einsum('kj,pkl->pjl', cosines, spectral, precision=PRECISE)
    return jnp.einsum('pjl,lm->pjm', row_pass, cosines, precision=PRECISE)

def forward_diff(source, dimension):
    extent = source.shape[dimension]
    ahead = lax.slice_in_dim(source, 1, extent, axis=dimension) - lax.slice_in_dim(source, 0, extent - 1, axis=dimension)
    return jnp.concatenate([ahead, jnp.zeros_like(lax.slice_in_dim(source, 0, 1, axis=dimension))], axis=dimension)

def adjoint_diff(flux, dimension):
    extent = flux.shape[dimension]
    earlier = jnp.concatenate([jnp.zeros_like(lax.slice_in_dim(flux, 0, 1, axis=dimension)), lax.slice_in_dim(flux, 0, extent - 1, axis=dimension)], axis=dimension)
    return earlier - flux

def regular(source, weights):
    divergence = jnp.zeros_like(source)
    for dimension in range(3):
        divergence = divergence + adjoint_diff(weights * forward_diff(source, dimension), dimension)
    return SMOOTHING * divergence

def reference(observed, estimate, spectrum):
    side_cells = observed.shape[1]
    cosines = cosine_block(0, side_cells, 0, side_cells, side_cells)
    observed_spectral = spectrum * forward(observed, cosines)
    squared = spectrum * spectrum
    current = estimate
    residual = observed
    for outer_step in range(SWEEPS):
        magnitude = jnp.zeros_like(current)
        for dimension in range(3):
            slope = forward_diff(current, dimension)
            magnitude = magnitude + slope * slope
        weights = 1.0 / jnp.maximum(jnp.sqrt(magnitude), HUBER_EDGE)
        residual = inverse(observed_spectral - squared * forward(current, cosines), cosines) - regular(current, weights)
        direction = residual
        norm_now = jnp.sum(residual * residual)
        for inner_step in range(ITERS):
            image = inverse(squared * forward(direction, cosines), cosines) + regular(direction, weights)
            step_len = norm_now / jnp.sum(direction * image)
            current = current + step_len * direction
            residual = residual - step_len * image
            norm_next = jnp.sum(residual * residual)
            direction = residual + norm_next / norm_now * direction
            norm_now = norm_next
    return (current, residual)
```

```python
import math

import jax
import jax.numpy as jnp
import numpy as np
from jax import lax
from jax.experimental import pallas as pl
from jax.experimental.pallas import tpu as pltpu
from jax.sharding import Mesh
from jax.sharding import PartitionSpec as P

PLANES = ("planes_0", "planes_1", "planes_2")
ROWS = ("rows_0", "rows_1")
ALL = PLANES + ROWS
N = 1024
R = 128
G = 8
HUBER_EDGE = 0.5
SMOOTHING = 0.3
F32 = jnp.float32
BF16 = jnp.bfloat16
VMEM = pl.BlockSpec(memory_space=pltpu.VMEM)
SMEM = pl.BlockSpec(memory_space=pltpu.SMEM)


def call(body, outs, name, flops, scratch=(), limit=24):
    def run(*args):
        size = sum(math.prod(a.shape) * a.dtype.itemsize for a in args)
        size += sum(math.prod(o.shape) * o.dtype.itemsize for o in outs)
        return pl.pallas_call(
            body,
            out_shape=tuple(outs),
            in_specs=[SMEM if a.dtype == jnp.int32 else VMEM for a in args],
            out_specs=tuple(VMEM for _ in outs),
            scratch_shapes=list(scratch),
            compiler_params=pltpu.CompilerParams(vmem_limit_bytes=limit << 20),
            cost_estimate=pl.CostEstimate(flops=flops, bytes_accessed=size, transcendentals=0),
            name=name,
        )(*args)

    return run


def shape(*dims, dtype=F32):
    return jax.ShapeDtypeStruct(dims, dtype)


def angle_tables():
    step = math.pi / (2.0 * N)
    coarse = np.arange(32)[:, None]
    fine = np.arange(32)[:, None]
    lane = np.arange(N)[None, :]
    norm = np.where(lane == 0, math.sqrt(1.0 / N), math.sqrt(2.0 / N))
    a_t = (lane * 64 * coarse) % (4 * N) * step
    b_t = (lane * (2 * fine + 1)) % (4 * N) * step
    sample_major = (np.cos(a_t), np.sin(a_t), np.cos(b_t) * norm, np.sin(b_t) * norm)
    odd = 2 * lane + 1
    a = (odd * 32 * coarse) % (4 * N) * step
    b = (odd * fine) % (4 * N) * step
    scale = math.sqrt(2.0 / N)
    freq_major = (np.cos(a), np.sin(a), np.cos(b) * scale, np.sin(b) * scale)
    return (
        np.stack(sample_major).astype(np.float32),
        np.stack(freq_major).astype(np.float32),
    )


def split(x):
    high = x.astype(BF16)
    low = (x - high.astype(F32)).astype(BF16)
    return high, low


def build_matrix(table, high, low, first_row):
    for a in range(32):
        rows = slice(32 * a, 32 * a + 32)
        value = table[0, a : a + 1, :] * table[2] - table[1, a : a + 1, :] * table[3]
        if first_row is not None and a == 0:
            row = lax.broadcasted_iota(jnp.int32, (32, N), 0)
            value = jnp.where(row == 0, first_row, value)
        high[rows, :], low[rows, :] = split(value)


def dot(a, b):
    return jnp.dot(a, b, preferred_element_type=F32)


def stacked_times(stack, rows, high, low, columns):
    both = dot(stack[0 : 2 * rows, :], high[:, columns])
    return both[:rows] + both[rows:] + dot(stack[0:rows, :], low[:, columns])


def matrix_times(high, low, rows, pair, width):
    both = dot(high[rows, :], pair[:, 0 : 2 * width])
    return both[:, :width] + both[:, width:] + dot(low[rows, :], pair[:, 0:width])


def first_kernel(observed, estimate, spectrum, table, sent, high, low, stack):
    build_matrix(table, high, low, None)
    stack[0:R, :], stack[2 * R : 3 * R, :] = split(observed[0])
    stack[R : 2 * R, :], stack[3 * R : 4 * R, :] = split(estimate[0])
    for d in range(G // 2):
        out = stacked_times(stack, 2 * R, high, low, slice(256 * d, 256 * d + 256))
        for h in range(2):
            lanes = slice(128 * h, 128 * h + 128)
            sent[2 * d + h, 0] = spectrum[0, :, 256 * d + 128 * h : 256 * d + 128 * h + 128]
            sent[2 * d + h, 1] = out[:R, lanes]
            sent[2 * d + h, 2] = out[R:, lanes]


def second_matrix_kernel(table, high, low):
    build_matrix(table, high, low, math.sqrt(1.0 / N))


def left(x):
    return pltpu.roll(x, N - 1, 1)


def weight_of(plane, row, value, last):
    column = jnp.where(last, 0.0, left(value) - value)
    square = plane * plane + row * row + column * column
    return 1.0 / jnp.maximum(jnp.sqrt(square), HUBER_EDGE)


def divergence(value, ahead_plane, behind_plane, ahead_row, behind_row, w_plane, w_back, w_row, w_row_back, w_col):
    flux_col = w_col * (left(value) - value)
    total = w_back * (value - behind_plane) - w_plane * (ahead_plane - value)
    total += w_row_back * (value - behind_row) - w_row * (ahead_row - value)
    total += pltpu.roll(flux_col, 1, 1) - flux_col
    return SMOOTHING * total


CHUNK = 16


def weights_kernel(
    place, estimate, behind, ahead, top, bottom, behind_bottom, ahead_top, high, low,
    reg, reg_sent, w_all, w_back_all, w_top, ext, ext_w, ext_back, stack,
):
    plane, row = place[0], place[1]
    ok_plane = jnp.where(plane < 15, 1.0, 0.0)
    ok_back = jnp.where(plane > 0, 1.0, 0.0)
    ok_top = jnp.where(row > 0, 1.0, 0.0)
    ok_bottom = jnp.where(row < G - 1, 1.0, 0.0)
    ext[7:8, :] = top[0]
    ext[8 : 8 + R, :] = estimate[0]
    ext[8 + R : 9 + R, :] = jnp.where(row < G - 1, bottom[0], estimate[0, R - 1 : R, :])
    ext_back[0:R, :] = behind[0]
    ext_back[R : R + 1, :] = jnp.where(row < G - 1, behind_bottom[0], behind[0, R - 1 : R, :])
    last1 = lax.broadcasted_iota(jnp.int32, (1, N), 1) == N - 1
    edge = ext[7:8, :]
    w_edge = weight_of(
        (ahead_top[0] - edge) * ok_plane, (ext[8:9, :] - edge) * ok_top, edge, last1
    ) * ok_top
    w_top[...] = w_edge
    ext_w[7:8, :] = w_edge
    last = lax.broadcasted_iota(jnp.int32, (CHUNK, N), 1) == N - 1
    for c in range(0, R, CHUNK):
        value = ext[8 + c : 8 + c + CHUNK, :]
        back = ext_back[c : c + CHUNK, :]
        w = weight_of(
            (ahead[0, c : c + CHUNK, :] - value) * ok_plane,
            ext[9 + c : 9 + c + CHUNK, :] - value,
            value,
            last,
        )
        ext_w[8 + c : 8 + c + CHUNK, :] = w
        w_all[c : c + CHUNK, :] = w
        w_back = weight_of(
            (value - back) * ok_back, ext_back[1 + c : 1 + c + CHUNK, :] - back, back, last
        ) * ok_back
        w_back_all[c : c + CHUNK, :] = w_back
    for c in range(0, R, CHUNK):
        value = ext[8 + c : 8 + c + CHUNK, :]
        w = ext_w[8 + c : 8 + c + CHUNK, :]
        out = divergence(
            value,
            ahead[0, c : c + CHUNK, :],
            behind[0, c : c + CHUNK, :],
            ext[9 + c : 9 + c + CHUNK, :],
            ext[7 + c : 7 + c + CHUNK, :],
            w * ok_plane,
            w_back_all[c : c + CHUNK, :],
            w,
            ext_w[7 + c : 7 + c + CHUNK, :],
            jnp.where(last, 0.0, w),
        )
        reg[c : c + CHUNK, :] = out
        stack[c : c + CHUNK, :], stack[R + c : R + c + CHUNK, :] = split(out)
    for d in range(G // 2):
        out = stacked_times(stack, R, high, low, slice(256 * d, 256 * d + 256))
        reg_sent[2 * d] = out[:, :128]
        reg_sent[2 * d + 1] = out[:, 128:]


def middle_kernel(got, reg_sent, f_high, f_low, s_high, s_low, sent, spectral, pair):
    for d in range(G):
        rows = slice(R * d, R * d + R)
        pair[rows, 0:128], pair[rows, 256:384] = split(got[d, 1])
        pair[rows, 128:256], pair[rows, 384:512] = split(got[d, 2])
    parts = []
    for m in range(4):
        rows = slice(256 * m, 256 * m + 256)
        out = matrix_times(f_high, f_low, rows, pair, 256)
        gain = jnp.concatenate([got[2 * m, 0], got[2 * m + 1, 0]], axis=0)
        spectral[rows, :] = gain * (out[:, :128] - gain * out[:, 128:])
    for d in range(G):
        rows = slice(R * d, R * d + R)
        pair[rows, 0:128], pair[rows, 128:256] = split(spectral[rows, :])
    for m in range(4):
        rows = slice(256 * m, 256 * m + 256)
        out = matrix_times(s_high, s_low, rows, pair, 128)
        parts.append(out)
        sent[2 * m, 0:R] = out[:R]
        sent[2 * m + 1, 0:R] = out[R:]
    for d in range(G):
        sent[d, R : R + 8] = jnp.zeros((8, 128), F32)
        sent[d, R + 8 :] = reg_sent[d]
    for d in range(G):
        if d > 0:
            sent[d, R : R + 1] = sent[d - 1, R - 1 : R]
        if d < G - 1:
            sent[d, R + 1 : R + 2] = sent[d + 1, 0:1]


def residual_kernel(got, reg, reg_top, reg_bottom, f_high, f_low, residual, edges, stack):
    rows = R + 16
    for d in range(G):
        lanes = slice(128 * d, 128 * d + 128)
        high, low = split(got[d, 0 : R + 8])
        pad = jnp.zeros((8, 128), BF16)
        stack[0:rows, lanes] = jnp.concatenate([high, pad], axis=0)
        stack[rows : 2 * rows, lanes] = jnp.concatenate([low, pad], axis=0)
    for d in range(G // 2):
        lanes = slice(256 * d, 256 * d + 256)
        out = stacked_times(stack, rows, f_high, f_low, lanes)
        residual[0, :, lanes] = out[:R] - reg[:, lanes]
        edges[0:1, lanes] = out[R : R + 1] - reg_top[0, :, lanes]
        edges[1:2, lanes] = out[R + 1 : R + 2] - reg_bottom[0, :, lanes]


def curvature_kernel(got, first, spectral, f_high, f_low, s_high, s_low, sent, total, pair):
    for d in range(G):
        rows = slice(R * d, R * d + R)
        pair[rows, 0:128], pair[rows, 128:256] = split(got[d, R + 8 :])
    acc = jnp.zeros((8, 128), F32)
    for m in range(4):
        rows = slice(256 * m, 256 * m + 256)
        out = spectral[rows, :] - matrix_times(f_high, f_low, rows, pair, 128)
        gain = jnp.concatenate([first[2 * m, 0], first[2 * m + 1, 0]], axis=0)
        scaled = gain * gain * out
        acc += jnp.sum((scaled * out).reshape(32, 8, 128), axis=0)
        pair[rows, 256:384], pair[rows, 384:512] = split(scaled)
    total[...] = acc
    for m in range(4):
        rows = slice(256 * m, 256 * m + 256)
        both = dot(s_high[rows, :], pair[:, 256:512])
        out = both[:, :128] + both[:, 128:] + dot(s_low[rows, :], pair[:, 256:384])
        sent[2 * m] = out[:R]
        sent[2 * m + 1] = out[R:]


def inner_kernel(
    place, residual, behind, ahead, edges, w_all, w_back_all, w_top, half_sent, total,
    reg, sent, ext, ext_w,
):
    plane, row = place[0], place[1]
    ok_plane = jnp.where(plane < 15, 1.0, 0.0)
    ext[7:8, :] = edges[0:1, :]
    ext[8 : 8 + R, :] = residual[0]
    ext[8 + R : 9 + R, :] = jnp.where(row < G - 1, edges[1:2, :], residual[0, R - 1 : R, :])
    ext_w[7:8, :] = w_top[...]
    ext_w[8 : 8 + R, :] = w_all[...]
    last = lax.broadcasted_iota(jnp.int32, (CHUNK, N), 1) == N - 1
    norm = jnp.zeros((8, N), F32)
    product = jnp.zeros((8, N), F32)
    for c in range(0, R, CHUNK):
        value = ext[8 + c : 8 + c + CHUNK, :]
        w = ext_w[8 + c : 8 + c + CHUNK, :]
        out = divergence(
            value,
            ahead[0, c : c + CHUNK, :],
            behind[0, c : c + CHUNK, :],
            ext[9 + c : 9 + c + CHUNK, :],
            ext[7 + c : 7 + c + CHUNK, :],
            w * ok_plane,
            w_back_all[c : c + CHUNK, :],
            w,
            ext_w[7 + c : 7 + c + CHUNK, :],
            jnp.where(last, 0.0, w),
        )
        reg[c : c + CHUNK, :] = out
        square = value * value
        cross = value * out
        norm += square[:8] + square[8:]
        product += cross[:8] + cross[8:]
    norm = jnp.sum(jnp.sum(norm, axis=0, keepdims=True).reshape(8, 128), axis=0, keepdims=True)
    product = jnp.sum(
        jnp.sum(product, axis=0, keepdims=True).reshape(8, 128) + total[...],
        axis=0, keepdims=True,
    )
    tile = jnp.concatenate([norm, product, jnp.zeros((6, 128), F32)], axis=0)
    for d in range(G):
        sent[d, 0:R] = half_sent[d]
        sent[d, R:] = tile


def image_kernel(got, reg, f_high, f_low, image, stack):
    for d in range(G):
        lanes = slice(128 * d, 128 * d + 128)
        stack[0:R, lanes], stack[R : 2 * R, lanes] = split(got[d, 0:R])
    for d in range(G // 2):
        lanes = slice(256 * d, 256 * d + 256)
        image[:, lanes] = stacked_times(stack, R, f_high, f_low, lanes) + reg[:, lanes]


def last_kernel(sums, estimate, residual, image, restored, final):
    tile = jnp.sum(sums[...], axis=0)
    norm = jnp.sum(tile[0:1, :], axis=1, keepdims=True)
    product = jnp.sum(tile[1:2, :], axis=1, keepdims=True)
    step = norm / product
    restored[0] = estimate[0] + step * residual[0]
    final[0] = residual[0] - step * image[...]


def across(x, axes):
    return lax.all_to_all(x, axes, split_axis=0, concat_axis=0, tiled=True)


def shards(observed, estimate, spectrum):
    planes, groups = 16, G
    place = jnp.stack([lax.axis_index(PLANES), lax.axis_index(ROWS)]).astype(jnp.int32)
    sample_table, freq_table = angle_tables()
    up = [(i, i + 1) for i in range(planes - 1)]
    down = [(i + 1, i) for i in range(planes - 1)]
    row_up = [(i, i + 1) for i in range(groups - 1)]
    row_down = [(i + 1, i) for i in range(groups - 1)]

    def device(p, r):
        return p * groups + r

    diagonal_from_behind = [
        (device(p - 1, r + 1), device(p, r)) for p in range(1, planes) for r in range(groups - 1)
    ]
    diagonal_from_ahead = [
        (device(p + 1, r - 1), device(p, r)) for p in range(planes - 1) for r in range(1, groups)
    ]
    matrix = shape(N, N, dtype=BF16)
    big = 2 * N * N * R

    sent, s_high, s_low = call(
        first_kernel,
        (shape(G, 3, R, 128), matrix, matrix),
        "first", 6 * big,
        (pltpu.VMEM((4 * R, N), BF16),),
    )(observed, estimate, spectrum, jnp.asarray(sample_table))
    first = across(sent, ROWS)

    f_high, f_low = call(second_matrix_kernel, (matrix, matrix), "matrix", 4 * N * N)(
        jnp.asarray(freq_table)
    )
    behind = lax.ppermute(estimate, PLANES, up)
    ahead = lax.ppermute(estimate, PLANES, down)
    head, tail = estimate[:, :1], estimate[:, R - 1 :]
    top = lax.ppermute(tail, ROWS, row_up)
    bottom = lax.ppermute(head, ROWS, row_down)
    behind_bottom = lax.ppermute(head, ALL, diagonal_from_behind)
    ahead_top = lax.ppermute(tail, ALL, diagonal_from_ahead)
    block = shape(R, N)
    reg, reg_sent, w_all, w_back, w_top = call(
        weights_kernel,
        (block, shape(G, R, 128), block, block, shape(1, N)),
        "weights", 3 * big,
        (
            pltpu.VMEM((R + 16, N), F32),
            pltpu.VMEM((R + 16, N), F32),
            pltpu.VMEM((R + 8, N), F32),
            pltpu.VMEM((2 * R, N), BF16),
        ),
    )(place, estimate, behind, ahead, top, bottom, behind_bottom, ahead_top, s_high, s_low)
    reg_top = lax.ppermute(reg[None, R - 1 :], ROWS, row_up)
    reg_bottom = lax.ppermute(reg[None, :1], ROWS, row_down)

    sent, spectral = call(
        middle_kernel,
        (shape(G, 2 * R + 8, 128), shape(N, 128)),
        "middle", 9 * big,
        (pltpu.VMEM((N, 512), BF16),),
    )(first, reg_sent, f_high, f_low, s_high, s_low)
    second = across(sent, ROWS)

    residual, edges = call(
        residual_kernel,
        (shape(1, R, N), shape(8, N)),
        "residual", 3 * big,
        (pltpu.VMEM((2 * R + 32, N), BF16),),
    )(second, reg, reg_top, reg_bottom, f_high, f_low)
    behind = lax.ppermute(residual, PLANES, up)
    ahead = lax.ppermute(residual, PLANES, down)
    half_sent, total = call(
        curvature_kernel,
        (shape(G, R, 128), shape(8, 128)),
        "curvature", 6 * big,
        (pltpu.VMEM((N, 512), BF16),),
    )(second, first, spectral, f_high, f_low, s_high, s_low)
    reg_residual, sent = call(
        inner_kernel,
        (block, shape(G, R + 8, 128)),
        "inner", big // 16,
        (pltpu.VMEM((R + 16, N), F32), pltpu.VMEM((R + 16, N), F32)),
    )(place, residual, behind, ahead, edges, w_all, w_back, w_top, half_sent, total)
    third = across(sent, ROWS)

    tile = jnp.sum(third[:, R:], axis=0)
    sums = across(jnp.broadcast_to(tile[None], (planes, 8, 128)), PLANES)
    image = call(
        image_kernel, (block,), "image", 3 * big, (pltpu.VMEM((2 * R, N), BF16),)
    )(third, reg_residual, f_high, f_low)[0]
    return call(last_kernel, (shape(1, R, N), shape(1, R, N)), "last", R * N * 4)(
        sums, estimate, residual, image
    )


def solution(mesh):
    finer = Mesh(
        mesh.devices.reshape(4, 2, 2, 2, 4),
        ("planes_0", "planes_1", "planes_2", "rows_0", "rows_1"),
    )
    spec = P(PLANES, ROWS, None)
    return jax.shard_map(
        shards,
        mesh=finer,
        in_specs=(spec, spec, spec),
        out_specs=(spec, spec),
        check_vma=False,
    )
```

```python
import math

import jax
import jax.numpy as jnp
from jax import lax
from jax.experimental import pallas as pl
from jax.experimental.pallas import tpu as pltpu
from jax.sharding import Mesh
from jax.sharding import PartitionSpec as P


PLANES = ("planes_0", "planes_1", "planes_2")
ROWS = ("rows_0", "rows_1")
N = 1024
R = 128
G = 8
HALO = R
EDGE = R + 8
REG = R + 16
HUBER_EDGE = 0.5
SMOOTHING = 0.3
F32 = jnp.float32
BF16 = jnp.bfloat16
VMEM = pl.BlockSpec(memory_space=pltpu.VMEM)
SMEM = pl.BlockSpec(memory_space=pltpu.SMEM)
ANY = pl.BlockSpec(memory_space=pl.ANY)
HBM = pl.BlockSpec(memory_space=pltpu.HBM)
DMA = pltpu.SemaphoreType.DMA
TABLE = pltpu.VMEM((4, 32, N), F32)
MATRIX = pltpu.VMEM((N, N), BF16)
CHUNK = 16


def shape(*dims, dtype=F32):
    return jax.ShapeDtypeStruct(dims, dtype)


def call(body, outs, flops, scratch=(), out_specs=None, aliases=None, limit=32):
    def place_of(a):
        if a.dtype == jnp.int32:
            return SMEM
        return ANY

    def launch(*args):
        size = sum(math.prod(a.shape) * a.dtype.itemsize for a in args)
        size += sum(math.prod(o.shape) * o.dtype.itemsize for o in outs)
        return pl.pallas_call(
            body,
            out_shape=tuple(outs),
            in_specs=[place_of(a) for a in args],
            out_specs=out_specs or tuple(VMEM for _ in outs),
            scratch_shapes=list(scratch),
            input_output_aliases=aliases or {},
            compiler_params=pltpu.CompilerParams(vmem_limit_bytes=limit << 20),
            cost_estimate=pl.CostEstimate(flops=flops, bytes_accessed=size, transcendentals=0),
        )(*args)

    return launch


def cos_sin(units):
    quarter = (units + 512) >> 10
    angle = (units - (quarter << 10)).astype(F32) * (math.pi / (2.0 * N))
    square = angle * angle
    sine = angle * (
        1.0 + square * (-1.0 / 6.0 + square * (1.0 / 120.0 + square * (-1.0 / 5040.0)))
    )
    cosine = 1.0 + square * (
        -0.5 + square * (1.0 / 24.0 + square * (-1.0 / 720.0 + square * (1.0 / 40320.0)))
    )
    odd = (quarter & 1) == 1
    cos_value = jnp.where(odd, sine, cosine)
    sin_value = jnp.where(odd, cosine, sine)
    cos_value = jnp.where(((quarter + 1) & 2) == 2, -cos_value, cos_value)
    sin_value = jnp.where((quarter & 2) == 2, -sin_value, sin_value)
    return cos_value, sin_value


def fill_table(table, samples):
    row = lax.broadcasted_iota(jnp.int32, (16, N), 0)
    lane = lax.broadcasted_iota(jnp.int32, (16, N), 1)
    if samples:
        shift = jnp.where(row < 5, row + 6, jnp.where(row < 10, row - 4, 0))
        value = lane
    else:
        shift = jnp.where(row < 5, row + 5, jnp.where(row < 10, row - 5, 0))
        value = 2 * lane + 1
    cos_bits, sin_bits = cos_sin((value << shift) & (4 * N - 1))
    norm = math.sqrt(2.0 / N)
    if samples:
        first = jnp.where(lane[:1] == 0, math.sqrt(1.0 / N), norm)
        fine = (cos_bits[10:11] * first, sin_bits[10:11] * first)
    else:
        fine = (jnp.full((1, N), norm, F32), jnp.zeros((1, N), F32))
    table[0, 0:1], table[1, 0:1] = jnp.ones((1, N), F32), jnp.zeros((1, N), F32)
    table[2, 0:1], table[3, 0:1] = fine
    for part in range(2):
        for bit in range(5):
            at = 5 * part + bit
            size = 1 << bit
            c, s = table[2 * part, 0:size], table[2 * part + 1, 0:size]
            cb, sb = cos_bits[at : at + 1], sin_bits[at : at + 1]
            table[2 * part, size : 2 * size] = c * cb - s * sb
            table[2 * part + 1, size : 2 * size] = s * cb + c * sb


def split(x):
    high = x.astype(BF16)
    low = (x - high.astype(F32)).astype(BF16)
    return high, low


def build(table, high, low, rows, lanes, first_row=None):
    for a in range(rows.start // 32, rows.stop // 32):
        value = table[0, a : a + 1, lanes] * table[2, :, lanes]
        value -= table[1, a : a + 1, lanes] * table[3, :, lanes]
        if first_row is not None and a == 0:
            row = lax.broadcasted_iota(jnp.int32, value.shape, 0)
            value = jnp.where(row == 0, first_row, value)
        block = slice(32 * a, 32 * a + 32)
        high[block, lanes], low[block, lanes] = split(value)


WHOLE = slice(0, N)


def build_samples(table, high, low, rows=WHOLE, lanes=WHOLE):
    build(table, high, low, rows, lanes)


def build_freqs(table, high, low, rows=WHOLE, lanes=WHOLE):
    build(table, high, low, rows, lanes, math.sqrt(1.0 / N))


def start(source, target, sem):
    copy = pltpu.make_async_copy(source, target, sem)
    copy.start()
    return copy


def dot(a, b):
    return jnp.dot(a, b, preferred_element_type=F32)


def stacked_times(stack, rows, high, low, columns):
    both = dot(stack[0 : 2 * rows, :], high[:, columns])
    return both[:rows] + both[rows:] + dot(stack[0:rows, :], low[:, columns])


def matrix_times(high, low, rows, pair, width, offset=0):
    both = dot(high[rows, :], pair[:, offset : offset + 2 * width])
    return both[:, :width] + both[:, width:] + dot(low[rows, :], pair[:, offset : offset + width])


def first_kernel(
    observed, estimate, spectrum, sent,
    table_v, observed_v, estimate_v, spectrum_v, sent_v, high, low, stack, sems,
):
    copies = [
        start(observed.at[0], observed_v, sems.at[1]),
        start(estimate.at[0], estimate_v, sems.at[2]),
        start(spectrum.at[0], spectrum_v, sems.at[3]),
    ]
    fill_table(table_v, True)
    copies[0].wait()
    stack[0:R, :], stack[2 * R : 3 * R, :] = split(observed_v[...])
    copies[1].wait()
    stack[R : 2 * R, :], stack[3 * R : 4 * R, :] = split(estimate_v[...])
    copies[2].wait()
    out_copies = []
    for d in range(G // 2):
        columns = slice(256 * d, 256 * d + 256)
        build_samples(table_v, high, low, WHOLE, columns)
        out = stacked_times(stack, 2 * R, high, low, columns)
        for h in range(2):
            lanes = slice(128 * h, 128 * h + 128)
            e = 2 * d + h
            sent_v[e, 0] = spectrum_v[:, 128 * e : 128 * e + 128]
            sent_v[e, 1] = out[:R, lanes]
            sent_v[e, 2] = out[R:, lanes]
        out_copies.append(
            start(sent_v.at[2 * d : 2 * d + 2], sent.at[2 * d : 2 * d + 2], sems.at[4 + d])
        )
    for copy in out_copies:
        copy.wait()


def left(x):
    return pltpu.roll(x, N - 1, 1)


def weight_of(plane, row, value, last):
    column = jnp.where(last, 0.0, left(value) - value)
    square = plane * plane + row * row + column * column
    return 1.0 / jnp.maximum(jnp.sqrt(square), HUBER_EDGE)


def divergence(value, ahead_plane, behind_plane, ahead_row, behind_row, w_plane, w_back, w_row, w_row_back, w_col):
    flux_col = w_col * (left(value) - value)
    total = w_back * (value - behind_plane) - w_plane * (ahead_plane - value)
    total += w_row_back * (value - behind_row) - w_row * (ahead_row - value)
    total += pltpu.roll(flux_col, 1, 1) - flux_col
    return SMOOTHING * total


def as_tile(row):
    return jnp.concatenate([row[:, 128 * i : 128 * i + 128] for i in range(8)], axis=0)


def weights_kernel(
    place, estimate, behind, ahead, from_above, from_below,
    reg, reg_sent, reg_rows, w_all, w_back_all, w_top,
    table_v, ext, ext_back, ahead_v, above_v, below_v, ext_w, high, low, stack, sems,
):
    copies = [
        start(estimate.at[0], ext.at[8 : 8 + R], sems.at[1]),
        start(behind.at[0], ext_back.at[0:R], sems.at[2]),
        start(ahead.at[0], ahead_v, sems.at[3]),
        start(from_above, above_v, sems.at[4]),
        start(from_below, below_v, sems.at[5]),
    ]
    fill_table(table_v, True)
    plane, row = place[0], place[1]
    ok_plane = jnp.where(plane < 15, 1.0, 0.0)
    ok_back = jnp.where(plane > 0, 1.0, 0.0)
    ok_top = jnp.where(row > 0, 1.0, 0.0)
    for copy in copies:
        copy.wait()
    ext[7:8, :] = above_v[0]
    ext[8 + R : 9 + R, :] = jnp.where(row < G - 1, below_v[0], ext[7 + R : 8 + R, :])
    ext_back[R : R + 1, :] = jnp.where(row < G - 1, below_v[1], ext_back[R - 1 : R, :])
    last1 = lax.broadcasted_iota(jnp.int32, (1, N), 1) == N - 1
    edge = ext[7:8, :]
    w_edge = weight_of(
        (above_v[1] - edge) * ok_plane, (ext[8:9, :] - edge) * ok_top, edge, last1
    ) * ok_top
    w_top[...] = w_edge
    ext_w[7:8, :] = w_edge
    last = lax.broadcasted_iota(jnp.int32, (CHUNK, N), 1) == N - 1
    for c in range(0, R, CHUNK):
        value = ext[8 + c : 8 + c + CHUNK, :]
        back = ext_back[c : c + CHUNK, :]
        w = weight_of(
            (ahead_v[c : c + CHUNK, :] - value) * ok_plane,
            ext[9 + c : 9 + c + CHUNK, :] - value,
            value,
            last,
        )
        ext_w[8 + c : 8 + c + CHUNK, :] = w
        w_all[c : c + CHUNK, :] = w
        w_back_all[c : c + CHUNK, :] = weight_of(
            (value - back) * ok_back, ext_back[1 + c : 1 + c + CHUNK, :] - back, back, last
        ) * ok_back
    for c in range(0, R, CHUNK):
        w = ext_w[8 + c : 8 + c + CHUNK, :]
        out = divergence(
            ext[8 + c : 8 + c + CHUNK, :],
            ahead_v[c : c + CHUNK, :],
            ext_back[c : c + CHUNK, :],
            ext[9 + c : 9 + c + CHUNK, :],
            ext[7 + c : 7 + c + CHUNK, :],
            w * ok_plane,
            w_back_all[c : c + CHUNK, :],
            w,
            ext_w[7 + c : 7 + c + CHUNK, :],
            jnp.where(last, 0.0, w),
        )
        reg[c : c + CHUNK, :] = out
        stack[c : c + CHUNK, :], stack[R + c : R + c + CHUNK, :] = split(out)
    reg_rows[0] = as_tile(reg[0:1, :])
    reg_rows[1] = as_tile(reg[R - 1 : R, :])
    for d in range(G // 2):
        columns = slice(256 * d, 256 * d + 256)
        build_samples(table_v, high, low, WHOLE, columns)
        out = stacked_times(stack, R, high, low, columns)
        reg_sent[2 * d] = out[:, :128]
        reg_sent[2 * d + 1] = out[:, 128:]


def middle_kernel(
    place, got, reg_sent, reg_rows, sent, spectral,
    freq_v, sample_v, got_v, rows_v, sent_v, f_high, f_low, s_high, s_low, pair, sems,
):
    copies = [
        start(got, got_v, sems.at[1]),
        start(reg_sent, sent_v.at[:, REG:], sems.at[3]),
        start(reg_rows, rows_v, sems.at[4]),
    ]
    row = place[1]
    fill_table(freq_v, False)
    fill_table(sample_v, True)
    copies[0].wait()
    for d in range(G):
        rows = slice(R * d, R * d + R)
        pair[rows, 0:128], pair[rows, 256:384] = split(got_v[d, 1])
        pair[rows, 128:256], pair[rows, 384:512] = split(got_v[d, 2])
    for m in range(4):
        rows = slice(256 * m, 256 * m + 256)
        build_freqs(freq_v, f_high, f_low, rows)
        out = matrix_times(f_high, f_low, rows, pair, 256)
        gain = jnp.concatenate([got_v[2 * m, 0], got_v[2 * m + 1, 0]], axis=0)
        value = gain * (out[:, :128] - gain * out[:, 128:])
        spectral[rows, :] = value
        pair[rows, 512:640], pair[rows, 640:768] = split(value)
    copies[2].wait()
    for d in range(G):
        sent_v[d, HALO:EDGE] = jnp.zeros((8, 128), F32)
        sent_v[d, EDGE:REG] = jnp.where(
            row == d - 1, rows_v[1], jnp.where(row == d + 1, rows_v[0], 0.0)
        )
    copies[1].wait()
    out_copies = []
    for m in range(4):
        rows = slice(256 * m, 256 * m + 256)
        build_samples(sample_v, s_high, s_low, rows)
        out = matrix_times(s_high, s_low, rows, pair, 128, 512)
        for h in range(2):
            d = 2 * m + h
            block = out[R * h : R * h + R]
            sent_v[d, 0:R] = block
            if d + 1 < G:
                sent_v[d + 1, HALO : HALO + 1] = block[R - 1 : R]
            if d > 0:
                sent_v[d - 1, HALO + 1 : HALO + 2] = block[0:1]
                out_copies.append(start(sent_v.at[d - 1], sent.at[d - 1], sems.at[5 + d - 1]))
    out_copies.append(start(sent_v.at[G - 1], sent.at[G - 1], sems.at[5 + G - 1]))
    for copy in out_copies:
        copy.wait()


def residual_kernel(
    place, got, reg, residual, edges,
    table_v, got_v, rows_v, reg_v, f_high, f_low, stack, sems,
):
    copies = [
        start(got.at[:, 0:REG], got_v, sems.at[1]),
        start(reg, reg_v, sems.at[2]),
    ]
    row = place[1]
    fill_table(table_v, False)
    for copy in copies:
        copy.wait()
    above = got_v[jnp.maximum(row - 1, 0), EDGE:REG, :]
    below = got_v[jnp.minimum(row + 1, G - 1), EDGE:REG, :]
    for i in range(G):
        rows_v[0:1, 128 * i : 128 * i + 128] = above[i : i + 1]
        rows_v[1:2, 128 * i : 128 * i + 128] = below[i : i + 1]
    rows = R + 16
    for d in range(G):
        lanes = slice(128 * d, 128 * d + 128)
        stack[0:rows, lanes], stack[rows : 2 * rows, lanes] = split(got_v[d])
    for d in range(G // 2):
        lanes = slice(256 * d, 256 * d + 256)
        build_freqs(table_v, f_high, f_low, WHOLE, lanes)
        out = stacked_times(stack, rows, f_high, f_low, lanes)
        residual[0, :, lanes] = out[:R] - reg_v[:, lanes]
        edges[0:2, lanes] = out[R : R + 2] - rows_v[0:2, lanes]


def curvature_kernel(
    got, first, spectral, sent, total,
    freq_v, sample_v, got_v, gain_v, spectral_v, sent_v, f_high, f_low, s_high, s_low, pair, sems,
):
    copies = [
        start(got.at[:, REG:], got_v, sems.at[1]),
        start(first.at[:, 0], gain_v, sems.at[3]),
        start(spectral, spectral_v, sems.at[4]),
    ]
    fill_table(freq_v, False)
    fill_table(sample_v, True)
    for copy in copies:
        copy.wait()
    for d in range(G):
        rows = slice(R * d, R * d + R)
        pair[rows, 0:128], pair[rows, 128:256] = split(got_v[d])
    acc = jnp.zeros((8, 128), F32)
    for m in range(4):
        rows = slice(256 * m, 256 * m + 256)
        build_freqs(freq_v, f_high, f_low, rows)
        out = spectral_v[rows, :] - matrix_times(f_high, f_low, rows, pair, 128)
        gain = jnp.concatenate([gain_v[2 * m], gain_v[2 * m + 1]], axis=0)
        scaled = gain * gain * out
        acc += jnp.sum((scaled * out).reshape(32, 8, 128), axis=0)
        pair[rows, 256:384], pair[rows, 384:512] = split(scaled)
    total[...] = acc
    out_copies = []
    for m in range(4):
        rows = slice(256 * m, 256 * m + 256)
        build_samples(sample_v, s_high, s_low, rows)
        out = matrix_times(s_high, s_low, rows, pair, 128, 256)
        sent_v[2 * m] = out[:R]
        sent_v[2 * m + 1] = out[R:]
        out_copies.append(
            start(sent_v.at[2 * m : 2 * m + 2], sent.at[2 * m : 2 * m + 2, 0:R], sems.at[5 + m])
        )
    for copy in out_copies:
        copy.wait()


def load_field(residual, edges, w_all, ext, ext_w, edges_v, sems):
    copies = [
        start(residual.at[0], ext.at[8 : 8 + R], sems.at[0]),
        start(edges, edges_v, sems.at[1]),
        start(w_all, ext_w.at[8 : 8 + R], sems.at[2]),
    ]
    return copies


def finish_field(place, copies, ext, edges_v):
    for copy in copies:
        copy.wait()
    row = place[1]
    ext[7:8, :] = edges_v[0:1, :]
    ext[8 + R : 9 + R, :] = jnp.where(row < G - 1, edges_v[1:2, :], ext[7 + R : 8 + R, :])


def product_kernel(
    place, residual, ahead, edges, w_all, total, half, sent,
    ext, ext_w, edges_v, ahead_v, total_v, tile_v, sems,
):
    copies = load_field(residual, edges, w_all, ext, ext_w, edges_v, sems)
    copies.append(start(ahead.at[0], ahead_v, sems.at[3]))
    copies.append(start(total, total_v, sems.at[4]))
    ok_plane = jnp.where(place[0] < 15, 1.0, 0.0)
    finish_field(place, copies, ext, edges_v)
    last = lax.broadcasted_iota(jnp.int32, (CHUNK, N), 1) == N - 1
    norm = jnp.zeros((8, N), F32)
    product = jnp.zeros((8, N), F32)
    for c in range(0, R, CHUNK):
        value = ext[8 + c : 8 + c + CHUNK, :]
        plane = (ahead_v[c : c + CHUNK, :] - value) * ok_plane
        row = ext[9 + c : 9 + c + CHUNK, :] - value
        column = jnp.where(last, 0.0, left(value) - value)
        cross = ext_w[8 + c : 8 + c + CHUNK, :] * (plane * plane + row * row + column * column)
        square = value * value
        norm += square[:8] + square[8:]
        product += cross[:8] + cross[8:]
    norm = jnp.sum(as_tile(jnp.sum(norm, axis=0, keepdims=True)), axis=0, keepdims=True)
    product = as_tile(SMOOTHING * jnp.sum(product, axis=0, keepdims=True)) + total_v[...]
    product = jnp.sum(product, axis=0, keepdims=True)
    tile_v[...] = jnp.concatenate([norm, product, jnp.zeros((6, 128), F32)], axis=0)
    out_copies = [start(tile_v, sent.at[d, R:], sems.at[5 + d]) for d in range(G)]
    for copy in out_copies:
        copy.wait()


def inner_kernel(
    place, residual, behind, ahead, edges, w_all, w_back_all, w_top, reg,
    ext, ext_w, edges_v, behind_v, ahead_v, back_v, sems,
):
    copies = load_field(residual, edges, w_all, ext, ext_w, edges_v, sems)
    copies += [
        start(behind.at[0], behind_v, sems.at[3]),
        start(ahead.at[0], ahead_v, sems.at[4]),
        start(w_back_all, back_v, sems.at[5]),
        start(w_top, ext_w.at[7:8], sems.at[6]),
    ]
    ok_plane = jnp.where(place[0] < 15, 1.0, 0.0)
    finish_field(place, copies, ext, edges_v)
    last = lax.broadcasted_iota(jnp.int32, (CHUNK, N), 1) == N - 1
    for c in range(0, R, CHUNK):
        w = ext_w[8 + c : 8 + c + CHUNK, :]
        reg[c : c + CHUNK, :] = divergence(
            ext[8 + c : 8 + c + CHUNK, :],
            ahead_v[c : c + CHUNK, :],
            behind_v[c : c + CHUNK, :],
            ext[9 + c : 9 + c + CHUNK, :],
            ext[7 + c : 7 + c + CHUNK, :],
            w * ok_plane,
            back_v[c : c + CHUNK, :],
            w,
            ext_w[7 + c : 7 + c + CHUNK, :],
            jnp.where(last, 0.0, w),
        )


def last_kernel(
    sums, got, reg, estimate, residual, restored, final,
    table_v, sums_v, got_v, reg_v, estimate_v, residual_v, restored_v, final_v,
    f_high, f_low, stack, sems,
):
    arrays = (
        (got.at[:, 0:R], got_v), (sums, sums_v), (reg, reg_v),
        (residual.at[0], residual_v), (estimate.at[0], estimate_v),
    )
    copies = [start(a, b, sems.at[i]) for i, (a, b) in enumerate(arrays)]
    fill_table(table_v, False)
    copies[0].wait()
    for d in range(G):
        lanes = slice(128 * d, 128 * d + 128)
        stack[0:R, lanes], stack[R : 2 * R, lanes] = split(got_v[d])
    for copy in copies[1:]:
        copy.wait()
    tile = jnp.sum(sums_v[...], axis=0)
    norm = jnp.sum(tile[0:1, :], axis=1, keepdims=True)
    product = jnp.sum(tile[1:2, :], axis=1, keepdims=True)
    step = norm / product
    restored_v[...] = estimate_v[...] + step * residual_v[...]
    out_copies = [start(restored_v, restored.at[0], sems.at[6])]
    for d in range(G // 2):
        lanes = slice(256 * d, 256 * d + 256)
        build_freqs(table_v, f_high, f_low, WHOLE, lanes)
        image = stacked_times(stack, R, f_high, f_low, lanes) + reg_v[:, lanes]
        final_v[:, lanes] = residual_v[:, lanes] - step * image
        out_copies.append(start(final_v.at[:, lanes], final.at[0, :, lanes], sems.at[7 + d]))
    for copy in out_copies:
        copy.wait()


def across(x, axes):
    return lax.all_to_all(x, axes, split_axis=0, concat_axis=0, tiled=True)


def field(rows=R):
    return pltpu.VMEM((rows, N), F32)


def step(observed, estimate, spectrum):
    planes, groups = 16, G
    place = jnp.stack([lax.axis_index(PLANES), lax.axis_index(ROWS)]).astype(jnp.int32)
    up = [(i, i + 1) for i in range(planes - 1)]
    down = [(i + 1, i) for i in range(planes - 1)]
    row_up = [(i, i + 1) for i in range(groups - 1)]
    row_down = [(i + 1, i) for i in range(groups - 1)]
    big = 2 * N * N * R
    block = shape(R, N)

    behind = lax.ppermute(estimate, PLANES, up)
    ahead = lax.ppermute(estimate, PLANES, down)
    sent = call(
        first_kernel,
        (shape(G, 3, R, 128),),
        6 * big,
        (TABLE, field(), field(), field(), pltpu.VMEM((G, 3, R, 128), F32), MATRIX, MATRIX,
         pltpu.VMEM((4 * R, N), BF16), DMA((8,))),
        (ANY,), limit=60,
    )(observed, estimate, spectrum)[0]
    first = across(sent, ROWS)

    tails = jnp.concatenate([estimate[:, R - 1 :], ahead[:, R - 1 :]], axis=0)
    heads = jnp.concatenate([estimate[:, :1], behind[:, :1]], axis=0)
    from_above = lax.ppermute(tails, ROWS, row_up)
    from_below = lax.ppermute(heads, ROWS, row_down)
    reg, reg_sent, reg_rows, w_all, w_back, w_top = call(
        weights_kernel,
        (block, shape(G, R, 128), shape(2, 8, 128), block, block, shape(1, N)),
        3 * big,
        (TABLE, field(R + 16), field(R + 8), field(), pltpu.VMEM((2, 1, N), F32),
         pltpu.VMEM((2, 1, N), F32), field(R + 16), MATRIX, MATRIX,
         pltpu.VMEM((2 * R, N), BF16), DMA((6,))),
    )(place, estimate, behind, ahead, from_above, from_below)

    sent, spectral = call(
        middle_kernel,
        (shape(G, REG + R, 128), shape(N, 128)),
        9 * big,
        (TABLE, TABLE, pltpu.VMEM((G, 3, R, 128), F32), pltpu.VMEM((2, 8, 128), F32),
         pltpu.VMEM((G, REG + R, 128), F32), MATRIX, MATRIX, MATRIX, MATRIX,
         pltpu.VMEM((N, 768), BF16), DMA((13,))),
        (ANY, VMEM),
    )(place, first, reg_sent, reg_rows)
    second = across(sent, ROWS)

    residual, edges = call(
        residual_kernel,
        (shape(1, R, N), shape(8, N)),
        3 * big,
        (TABLE, pltpu.VMEM((G, REG, 128), F32), field(8), field(), MATRIX, MATRIX,
         pltpu.VMEM((2 * R + 32, N), BF16), DMA((3,))),
    )(place, second, reg)
    ahead = lax.ppermute(residual, PLANES, down)
    half_sent, total = call(
        curvature_kernel,
        (shape(G, R + 8, 128), shape(8, 128)),
        6 * big,
        (TABLE, TABLE, pltpu.VMEM((G, R, 128), F32), pltpu.VMEM((G, R, 128), F32),
         pltpu.VMEM((N, 128), F32), pltpu.VMEM((G, R, 128), F32), MATRIX, MATRIX, MATRIX, MATRIX,
         pltpu.VMEM((N, 512), BF16), DMA((9,))),
        (ANY, VMEM),
    )(second, first, spectral)
    sent = call(
        product_kernel,
        (shape(G, R + 8, 128),),
        big // 16,
        (field(R + 16), field(R + 16), field(8), field(), pltpu.VMEM((8, 128), F32),
         pltpu.VMEM((8, 128), F32), DMA((13,))),
        (ANY,),
        {6: 0},
    )(place, residual, ahead, edges, w_all, total, half_sent)[0]
    third = across(sent, ROWS)

    late, _ = lax.optimization_barrier((residual, ahead))
    behind = lax.ppermute(late, PLANES, up)
    reg_residual = call(
        inner_kernel,
        (block,),
        big // 16,
        (field(R + 16), field(R + 16), field(8), field(), field(), field(), DMA((7,))),
    )(place, residual, behind, ahead, edges, w_all, w_back, w_top)[0]

    tile = jnp.sum(third[:, R:], axis=0)
    sums = across(jnp.broadcast_to(tile[None], (planes, 8, 128)), PLANES)
    return call(
        last_kernel,
        (shape(1, R, N), shape(1, R, N)),
        3 * big,
        (TABLE, pltpu.VMEM((16, 8, 128), F32), pltpu.VMEM((G, R, 128), F32), field(), field(),
         field(), field(), field(), MATRIX, MATRIX, pltpu.VMEM((2 * R, N), BF16), DMA((11,))),
        (ANY, ANY),
    )(sums, third, reg_residual, estimate, residual)


def solution(mesh):
    finer = Mesh(
        mesh.devices.reshape(4, 2, 2, 2, 4),
        ("planes_0", "planes_1", "planes_2", "rows_0", "rows_1"),
    )
    spec = P(PLANES, ROWS, None)
    return jax.shard_map(
        step,
        mesh=finer,
        in_specs=(spec, spec, spec),
        out_specs=(spec, spec),
        check_vma=False,
    )
```

```python
import math

import jax
import jax.numpy as jnp
from jax import lax
from jax.experimental import pallas as pl
from jax.experimental.pallas import tpu as pltpu
from jax.sharding import Mesh
from jax.sharding import PartitionSpec as P


PLANES = ("planes_0", "planes_1", "planes_2")
ROWS = ("rows_0", "rows_1")
ALL = PLANES + ROWS
N = 1024
R = 128
G = 8
SECOND = R + 8
BOTH = 2 * R + 8
HUBER_EDGE = 0.5
SMOOTHING = 0.3
F32 = jnp.float32
BF16 = jnp.bfloat16
VMEM = pl.BlockSpec(memory_space=pltpu.VMEM)
SMEM = pl.BlockSpec(memory_space=pltpu.SMEM)
ANY = pl.BlockSpec(memory_space=pl.ANY)
HBM = pl.BlockSpec(memory_space=pltpu.HBM)
DMA = pltpu.SemaphoreType.DMA
TABLE = pltpu.VMEM((4, 32, N), F32)
MATRIX = pltpu.VMEM((N, N), BF16)
CHUNK = 16


def shape(*dims, dtype=F32):
    return jax.ShapeDtypeStruct(dims, dtype)


def call(body, outs, flops, scratch=(), out_specs=None, aliases=None, limit=32, direct=0):
    def place_of(i, a):
        if a.dtype == jnp.int32:
            return SMEM
        return VMEM if i < direct else ANY

    def launch(*args):
        size = sum(math.prod(a.shape) * a.dtype.itemsize for a in args)
        size += sum(math.prod(o.shape) * o.dtype.itemsize for o in outs)
        return pl.pallas_call(
            body,
            out_shape=tuple(outs),
            in_specs=[place_of(i, a) for i, a in enumerate(args)],
            out_specs=out_specs or tuple(VMEM for _ in outs),
            scratch_shapes=list(scratch),
            input_output_aliases=aliases or {},
            compiler_params=pltpu.CompilerParams(vmem_limit_bytes=limit << 20),
            cost_estimate=pl.CostEstimate(flops=flops, bytes_accessed=size, transcendentals=0),
        )(*args)

    return launch


def cos_sin(units):
    quarter = (units + 512) >> 10
    angle = (units - (quarter << 10)).astype(F32) * (math.pi / (2.0 * N))
    square = angle * angle
    sine = angle * (
        1.0 + square * (-1.0 / 6.0 + square * (1.0 / 120.0 + square * (-1.0 / 5040.0)))
    )
    cosine = 1.0 + square * (
        -0.5 + square * (1.0 / 24.0 + square * (-1.0 / 720.0 + square * (1.0 / 40320.0)))
    )
    odd = (quarter & 1) == 1
    cos_value = jnp.where(odd, sine, cosine)
    sin_value = jnp.where(odd, cosine, sine)
    cos_value = jnp.where(((quarter + 1) & 2) == 2, -cos_value, cos_value)
    sin_value = jnp.where((quarter & 2) == 2, -sin_value, sin_value)
    return cos_value, sin_value


def fill_table(table, samples):
    row = lax.broadcasted_iota(jnp.int32, (16, N), 0)
    lane = lax.broadcasted_iota(jnp.int32, (16, N), 1)
    if samples:
        shift = jnp.where(row < 5, row + 6, jnp.where(row < 10, row - 4, 0))
        value = lane
    else:
        shift = jnp.where(row < 5, row + 5, jnp.where(row < 10, row - 5, 0))
        value = 2 * lane + 1
    cos_bits, sin_bits = cos_sin((value << shift) & (4 * N - 1))
    norm = math.sqrt(2.0 / N)
    if samples:
        first = jnp.where(lane[:1] == 0, math.sqrt(1.0 / N), norm)
        fine = (cos_bits[10:11] * first, sin_bits[10:11] * first)
    else:
        fine = (jnp.full((1, N), norm, F32), jnp.zeros((1, N), F32))
    table[0, 0:1], table[1, 0:1] = jnp.ones((1, N), F32), jnp.zeros((1, N), F32)
    table[2, 0:1], table[3, 0:1] = fine
    for part in range(2):
        for bit in range(5):
            at = 5 * part + bit
            size = 1 << bit
            c, s = table[2 * part, 0:size], table[2 * part + 1, 0:size]
            cb, sb = cos_bits[at : at + 1], sin_bits[at : at + 1]
            table[2 * part, size : 2 * size] = c * cb - s * sb
            table[2 * part + 1, size : 2 * size] = s * cb + c * sb


def split(x):
    high = x.astype(BF16)
    low = (x - high.astype(F32)).astype(BF16)
    return high, low


def build(table, high, low, rows, lanes, first_row=None):
    for a in range(rows.start // 32, rows.stop // 32):
        value = table[0, a : a + 1, lanes] * table[2, :, lanes]
        value -= table[1, a : a + 1, lanes] * table[3, :, lanes]
        if first_row is not None and a == 0:
            row = lax.broadcasted_iota(jnp.int32, value.shape, 0)
            value = jnp.where(row == 0, first_row, value)
        block = slice(32 * a, 32 * a + 32)
        high[block, lanes], low[block, lanes] = split(value)


WHOLE = slice(0, N)


def build_samples(table, high, low, rows=WHOLE, lanes=WHOLE):
    build(table, high, low, rows, lanes)


def build_freqs(table, high, low, rows=WHOLE, lanes=WHOLE):
    build(table, high, low, rows, lanes, math.sqrt(1.0 / N))


def start(source, target, sem):
    copy = pltpu.make_async_copy(source, target, sem)
    copy.start()
    return copy


def dot(a, b):
    return jnp.dot(a, b, preferred_element_type=F32)


def stacked_times(stack, rows, high, low, columns):
    both = dot(stack[0 : 2 * rows, :], high[:, columns])
    return both[:rows] + both[rows:] + dot(stack[0:rows, :], low[:, columns])


def matrix_times(high, low, rows, pair, width, offset=0):
    both = dot(high[rows, :], pair[:, offset : offset + 2 * width])
    return both[:, :width] + both[:, width:] + dot(low[rows, :], pair[:, offset : offset + width])


def first_kernel(
    observed, estimate, sent,
    table_v, observed_v, estimate_v, sent_v, high, low, stack, sems,
):
    copies = [
        start(observed.at[0], observed_v, sems.at[1]),
        start(estimate.at[0], estimate_v, sems.at[2]),
    ]
    fill_table(table_v, True)
    copies[0].wait()
    stack[0:R, :], stack[2 * R : 3 * R, :] = split(observed_v[...])
    copies[1].wait()
    stack[R : 2 * R, :], stack[3 * R : 4 * R, :] = split(estimate_v[...])
    out_copies = []
    for d in range(G // 2):
        columns = slice(256 * d, 256 * d + 256)
        build_samples(table_v, high, low, WHOLE, columns)
        out = stacked_times(stack, 2 * R, high, low, columns)
        for h in range(2):
            lanes = slice(128 * h, 128 * h + 128)
            e = 2 * d + h
            sent_v[e, 0] = out[:R, lanes]
            sent_v[e, 1] = out[R:, lanes]
        out_copies.append(
            start(sent_v.at[2 * d : 2 * d + 2], sent.at[2 * d : 2 * d + 2], sems.at[4 + d])
        )
    for copy in out_copies:
        copy.wait()


def left(x):
    return pltpu.roll(x, N - 1, 1)


def weight_of(plane, row, value, last):
    column = jnp.where(last, 0.0, left(value) - value)
    square = plane * plane + row * row + column * column
    return 1.0 / jnp.maximum(jnp.sqrt(square), HUBER_EDGE)


def divergence(value, ahead_plane, behind_plane, ahead_row, behind_row, w_plane, w_back, w_row, w_row_back, w_col):
    flux_col = w_col * (left(value) - value)
    total = w_back * (value - behind_plane) - w_plane * (ahead_plane - value)
    total += w_row_back * (value - behind_row) - w_row * (ahead_row - value)
    total += pltpu.roll(flux_col, 1, 1) - flux_col
    return SMOOTHING * total


def as_tile(row):
    return jnp.concatenate([row[:, 128 * i : 128 * i + 128] for i in range(8)], axis=0)


def weights_kernel(
    place, estimate, behind, ahead, from_above, from_below, spectrum,
    sent, w_all, w_back_all, w_top,
    table_v, ext, ext_back, spectrum_v, sent_v, ext_w,
    high, low, stack, sems,
):
    spectrum_copy = start(spectrum.at[0], spectrum_v, sems.at[0])
    fill_table(table_v, True)
    plane, row = place[0], place[1]
    ok_plane = jnp.where(plane < 15, 1.0, 0.0)
    ok_back = jnp.where(plane > 0, 1.0, 0.0)
    ok_top = jnp.where(row > 0, 1.0, 0.0)
    ext[8 : 8 + R, :] = estimate[0]
    ext_back[0:R, :] = behind[0]
    ext[7:8, :] = from_above[0]
    ext[8 + R : 9 + R, :] = jnp.where(row < G - 1, from_below[0], estimate[0, R - 1 : R, :])
    ext_back[R : R + 1, :] = jnp.where(row < G - 1, from_below[1], behind[0, R - 1 : R, :])
    last1 = lax.broadcasted_iota(jnp.int32, (1, N), 1) == N - 1
    edge = ext[7:8, :]
    w_edge = weight_of(
        (from_above[1] - edge) * ok_plane, (ext[8:9, :] - edge) * ok_top, edge, last1
    ) * ok_top
    w_top[...] = w_edge
    ext_w[7:8, :] = w_edge
    last = lax.broadcasted_iota(jnp.int32, (CHUNK, N), 1) == N - 1
    for c in range(0, R, CHUNK):
        value = ext[8 + c : 8 + c + CHUNK, :]
        back = ext_back[c : c + CHUNK, :]
        w = weight_of(
            (ahead[0, c : c + CHUNK, :] - value) * ok_plane,
            ext[9 + c : 9 + c + CHUNK, :] - value,
            value,
            last,
        )
        ext_w[8 + c : 8 + c + CHUNK, :] = w
        w_all[c : c + CHUNK, :] = w
        w_back_all[c : c + CHUNK, :] = weight_of(
            (value - back) * ok_back, ext_back[1 + c : 1 + c + CHUNK, :] - back, back, last
        ) * ok_back
    for c in range(0, R, CHUNK):
        w = ext_w[8 + c : 8 + c + CHUNK, :]
        out = divergence(
            ext[8 + c : 8 + c + CHUNK, :],
            ahead[0, c : c + CHUNK, :],
            ext_back[c : c + CHUNK, :],
            ext[9 + c : 9 + c + CHUNK, :],
            ext[7 + c : 7 + c + CHUNK, :],
            w * ok_plane,
            w_back_all[c : c + CHUNK, :],
            w,
            ext_w[7 + c : 7 + c + CHUNK, :],
            jnp.where(last, 0.0, w),
        )
        stack[c : c + CHUNK, :], stack[R + c : R + c + CHUNK, :] = split(out)
    spectrum_copy.wait()
    out_copies = []
    for d in range(G // 2):
        columns = slice(256 * d, 256 * d + 256)
        build_samples(table_v, high, low, WHOLE, columns)
        out = stacked_times(stack, R, high, low, columns)
        for h in range(2):
            e = 2 * d + h
            sent_v[e, 0] = spectrum_v[:, 128 * e : 128 * e + 128]
            sent_v[e, 1] = out[:, 128 * h : 128 * h + 128]
        out_copies.append(
            start(sent_v.at[2 * d : 2 * d + 2], sent.at[2 * d : 2 * d + 2], sems.at[1 + d])
        )
    for copy in out_copies:
        copy.wait()


def forward_kernel(got, spectral, table_v, high, low, pair):
    fill_table(table_v, False)
    for d in range(G):
        rows = slice(R * d, R * d + R)
        pair[rows, 0:128], pair[rows, 256:384] = split(got[d, 0])
        pair[rows, 128:256], pair[rows, 384:512] = split(got[d, 1])
    for m in range(4):
        rows = slice(256 * m, 256 * m + 256)
        build_freqs(table_v, high, low, rows)
        spectral[rows, :] = matrix_times(high, low, rows, pair, 256)


def middle_kernel(
    got, spectral, sent, freq_v, sample_v, f_high, f_low, s_high, s_low, pair,
):
    fill_table(freq_v, False)
    fill_table(sample_v, True)
    for d in range(G):
        rows = slice(R * d, R * d + R)
        pair[rows, 0:128], pair[rows, 128:256] = split(got[d, 1])
    for m in range(4):
        rows = slice(256 * m, 256 * m + 256)
        build_freqs(freq_v, f_high, f_low, rows)
        reg = matrix_times(f_high, f_low, rows, pair, 128)
        gain = jnp.concatenate([got[2 * m, 0], got[2 * m + 1, 0]], axis=0)
        value = gain * (spectral[rows, :128] - gain * spectral[rows, 128:]) - reg
        pair[rows, 256:384], pair[rows, 512:640] = split(value)
        pair[rows, 384:512], pair[rows, 640:768] = split(gain * gain * value)
    for d in range(G):
        sent[d, R:SECOND] = jnp.zeros((8, 128), F32)
    for m in range(4):
        rows = slice(256 * m, 256 * m + 256)
        build_samples(sample_v, s_high, s_low, rows)
        out = matrix_times(s_high, s_low, rows, pair, 256, 256)
        for h in range(2):
            d = 2 * m + h
            block = out[R * h : R * h + R]
            sent[d, 0:R] = block[:, :128]
            sent[d, SECOND:] = block[:, 128:]
            if d + 1 < G:
                sent[d + 1, R : R + 1] = block[R - 1 : R, :128]
            if d > 0:
                sent[d - 1, R + 1 : R + 2] = block[0:1, :128]


def residual_kernel(got, residual, image, edges, table_v, f_high, f_low, stack):
    fill_table(table_v, False)
    rows = BOTH + 8
    pad = jnp.zeros((8, 128), BF16)
    for d in range(G):
        lanes = slice(128 * d, 128 * d + 128)
        high, low = split(got[d])
        stack[0:rows, lanes] = jnp.concatenate([high, pad], axis=0)
        stack[rows : 2 * rows, lanes] = jnp.concatenate([low, pad], axis=0)
    for d in range(G // 2):
        lanes = slice(256 * d, 256 * d + 256)
        build_freqs(table_v, f_high, f_low, WHOLE, lanes)
        out = stacked_times(stack, rows, f_high, f_low, lanes)
        residual[0, :, lanes] = out[:R]
        edges[0:2, lanes] = out[R : R + 2]
        image[:, lanes] = out[SECOND:BOTH]


def extend(place, residual, edges, ext):
    ext[7:8, :] = edges[0:1, :]
    ext[8 : 8 + R, :] = residual[0]
    ext[8 + R : 9 + R, :] = jnp.where(place[1] < G - 1, edges[1:2, :], residual[0, R - 1 : R, :])


def partial_kernel(place, residual, edges, w_all, image, parts, ext):
    extend(place, residual, edges, ext)
    last = lax.broadcasted_iota(jnp.int32, (CHUNK, N), 1) == N - 1
    norm = jnp.zeros((8, N), F32)
    product = jnp.zeros((8, N), F32)
    for c in range(0, R, CHUNK):
        value = ext[8 + c : 8 + c + CHUNK, :]
        row = ext[9 + c : 9 + c + CHUNK, :] - value
        column = jnp.where(last, 0.0, left(value) - value)
        cross = (SMOOTHING * w_all[c : c + CHUNK, :]) * (row * row + column * column)
        cross += value * image[c : c + CHUNK, :]
        square = value * value
        norm += square[:8] + square[8:]
        product += cross[:8] + cross[8:]
    parts[0] = norm
    parts[1] = product


def product_kernel(place, residual, ahead, w_all, parts, sent):
    total = jnp.zeros((8, N), F32)
    for c in range(0, R, CHUNK):
        plane = ahead[0, c : c + CHUNK, :] - residual[0, c : c + CHUNK, :]
        cross = w_all[c : c + CHUNK, :] * (plane * plane)
        total += cross[:8] + cross[8:]
    product = parts[1] + jnp.where(place[0] < 15, SMOOTHING, 0.0) * total
    norm = jnp.sum(as_tile(jnp.sum(parts[0], axis=0, keepdims=True)), axis=0, keepdims=True)
    product = jnp.sum(as_tile(jnp.sum(product, axis=0, keepdims=True)), axis=0, keepdims=True)
    lane = lax.broadcasted_iota(jnp.int32, (1, 128), 1)
    both = jnp.where(
        lane < 64, norm + pltpu.roll(norm, 64, 1), product + pltpu.roll(product, 64, 1)
    )
    sent[...] = jnp.broadcast_to(both[None], (128, 1, 128))


def inner_kernel(
    place, residual, behind, ahead, edges, w_all, w_back_all, w_top, blurred, image, ext, ext_w,
):
    ok_plane = jnp.where(place[0] < 15, 1.0, 0.0)
    extend(place, residual, edges, ext)
    ext_w[7:8, :] = w_top[...]
    ext_w[8 : 8 + R, :] = w_all[...]
    last = lax.broadcasted_iota(jnp.int32, (CHUNK, N), 1) == N - 1
    for c in range(0, R, CHUNK):
        w = ext_w[8 + c : 8 + c + CHUNK, :]
        image[c : c + CHUNK, :] = blurred[c : c + CHUNK, :] + divergence(
            ext[8 + c : 8 + c + CHUNK, :],
            ahead[0, c : c + CHUNK, :],
            behind[0, c : c + CHUNK, :],
            ext[9 + c : 9 + c + CHUNK, :],
            ext[7 + c : 7 + c + CHUNK, :],
            w * ok_plane,
            w_back_all[c : c + CHUNK, :],
            w,
            ext_w[7 + c : 7 + c + CHUNK, :],
            jnp.where(last, 0.0, w),
        )


def last_kernel(
    sums, estimate, residual, image, restored, final, restored_v, final_v, sems,
):
    both = jnp.sum(sums[...], axis=0)
    lane = lax.broadcasted_iota(jnp.int32, (1, 128), 1)
    norm = jnp.sum(jnp.where(lane < 64, both, 0.0), axis=1, keepdims=True)
    product = jnp.sum(jnp.where(lane < 64, 0.0, both), axis=1, keepdims=True)
    step = norm / product
    out_copies = []
    for c in range(4):
        rows = slice(32 * c, 32 * c + 32)
        restored_v[rows] = estimate[0, rows] + step * residual[0, rows]
        out_copies.append(start(restored_v.at[rows], restored.at[0, rows], sems.at[2 * c]))
        final_v[rows] = residual[0, rows] - step * image[rows]
        out_copies.append(start(final_v.at[rows], final.at[0, rows], sems.at[2 * c + 1]))
    for copy in out_copies:
        copy.wait()


def across(x, axes):
    return lax.all_to_all(x, axes, split_axis=0, concat_axis=0, tiled=True)


def field(rows=R):
    return pltpu.VMEM((rows, N), F32)


def step(observed, estimate, spectrum):
    planes, groups = 16, G
    place = jnp.stack([lax.axis_index(PLANES), lax.axis_index(ROWS)]).astype(jnp.int32)
    up = [(i, i + 1) for i in range(planes - 1)]
    down = [(i + 1, i) for i in range(planes - 1)]
    row_up = [(i, i + 1) for i in range(groups - 1)]
    row_down = [(i + 1, i) for i in range(groups - 1)]
    big = 2 * N * N * R
    block = shape(R, N)

    behind = lax.ppermute(estimate, PLANES, up)
    ahead = lax.ppermute(estimate, PLANES, down)
    sent = call(
        first_kernel,
        (shape(G, 2, R, 128),),
        6 * big,
        (TABLE, field(), field(), pltpu.VMEM((G, 2, R, 128), F32), MATRIX, MATRIX,
         pltpu.VMEM((4 * R, N), BF16), DMA((8,))),
        (ANY,), limit=60,
    )(observed, estimate)[0]
    first = across(sent, ROWS)

    tails = jnp.concatenate([estimate[:, R - 1 :], ahead[:, R - 1 :]], axis=0)
    heads = jnp.concatenate([estimate[:, :1], behind[:, :1]], axis=0)
    from_above = lax.ppermute(tails, ROWS, row_up)
    from_below = lax.ppermute(heads, ROWS, row_down)
    sent, w_all, w_back, w_top = call(
        weights_kernel,
        (shape(G, 2, R, 128), block, block, shape(1, N)),
        3 * big,
        (TABLE, field(R + 16), field(R + 8), field(), pltpu.VMEM((G, 2, R, 128), F32),
         field(R + 16), MATRIX, MATRIX, pltpu.VMEM((2 * R, N), BF16), DMA((5,))),
        (ANY, VMEM, VMEM, VMEM), direct=6,
    )(place, estimate, behind, ahead, from_above, from_below, spectrum)
    second = across(sent, ROWS)
    spectral = call(
        forward_kernel,
        (shape(N, 256),),
        6 * big,
        (TABLE, MATRIX, MATRIX, pltpu.VMEM((N, 512), BF16)),
        direct=9,
    )(first)[0]
    sent = call(
        middle_kernel,
        (shape(G, BOTH, 128),),
        9 * big,
        (TABLE, TABLE, MATRIX, MATRIX, MATRIX, MATRIX, pltpu.VMEM((N, 768), BF16)),
        direct=9,
    )(second, spectral)[0]
    third = across(sent, ROWS)

    residual, blurred, edges = call(
        residual_kernel,
        (shape(1, R, N), block, shape(8, N)),
        6 * big,
        (TABLE, MATRIX, MATRIX, pltpu.VMEM((2 * BOTH + 16, N), BF16)),
        direct=9,
    )(third)
    ahead = lax.ppermute(residual, PLANES, down)
    parts = call(
        partial_kernel, (shape(2, 8, N),), big // 16, (field(R + 16),), direct=9
    )(place, residual, edges, w_all, blurred)[0]
    late, _ = lax.optimization_barrier((residual, parts))
    behind = lax.ppermute(late, PLANES, up)
    sent = call(
        product_kernel, (shape(128, 1, 128),), big // 64, direct=9
    )(place, residual, ahead, w_all, parts)[0]
    sums = across(sent, ALL)
    image = call(
        inner_kernel, (block,), big // 16, (field(R + 16), field(R + 16)), direct=9
    )(place, residual, behind, ahead, edges, w_all, w_back, w_top, blurred)[0]
    return call(
        last_kernel,
        (shape(1, R, N), shape(1, R, N)),
        R * N * 4,
        (field(), field(), DMA((8,))),
        (ANY, ANY),
        direct=9,
    )(sums, estimate, residual, image)


def solution(mesh):
    finer = Mesh(
        mesh.devices.reshape(4, 2, 2, 2, 4),
        ("planes_0", "planes_1", "planes_2", "rows_0", "rows_1"),
    )
    spec = P(PLANES, ROWS, None)
    return jax.shard_map(
        step,
        mesh=finer,
        in_specs=(spec, spec, spec),
        out_specs=(spec, spec),
        check_vma=False,
    )
```

```python
import math

import jax
import jax.numpy as jnp
from jax import lax
from jax.experimental import pallas as pl
from jax.experimental.pallas import tpu as pltpu
from jax.sharding import Mesh
from jax.sharding import PartitionSpec as P


PLANES = ("planes_0", "planes_1", "planes_2")
ROWS = ("rows_0", "rows_1")
ALL = PLANES + ROWS
N = 1024
R = 128
G = 8
SECOND = R + 8
BOTH = 2 * R + 8
HUBER_EDGE = 0.5
SMOOTHING = 0.3
F32 = jnp.float32
BF16 = jnp.bfloat16
VMEM = pl.BlockSpec(memory_space=pltpu.VMEM)
SMEM = pl.BlockSpec(memory_space=pltpu.SMEM)
ANY = pl.BlockSpec(memory_space=pl.ANY)
HBM = pl.BlockSpec(memory_space=pltpu.HBM)
DMA = pltpu.SemaphoreType.DMA
TABLE = pltpu.VMEM((4, 32, N), F32)
MATRIX = pltpu.VMEM((N, N), BF16)
CHUNK = 16


def shape(*dims, dtype=F32):
    return jax.ShapeDtypeStruct(dims, dtype)


def call(body, outs, flops, scratch=(), out_specs=None, aliases=None, limit=32, direct=0):
    def place_of(i, a):
        if a.dtype == jnp.int32:
            return SMEM
        return VMEM if i < direct else ANY

    def launch(*args):
        size = sum(math.prod(a.shape) * a.dtype.itemsize for a in args)
        size += sum(math.prod(o.shape) * o.dtype.itemsize for o in outs)
        return pl.pallas_call(
            body,
            out_shape=tuple(outs),
            in_specs=[place_of(i, a) for i, a in enumerate(args)],
            out_specs=out_specs or tuple(VMEM for _ in outs),
            scratch_shapes=list(scratch),
            input_output_aliases=aliases or {},
            compiler_params=pltpu.CompilerParams(vmem_limit_bytes=limit << 20),
            cost_estimate=pl.CostEstimate(flops=flops, bytes_accessed=size, transcendentals=0),
        )(*args)

    return launch


def cos_sin(units):
    quarter = (units + 512) >> 10
    angle = (units - (quarter << 10)).astype(F32) * (math.pi / (2.0 * N))
    square = angle * angle
    sine = angle * (
        1.0 + square * (-1.0 / 6.0 + square * (1.0 / 120.0 + square * (-1.0 / 5040.0)))
    )
    cosine = 1.0 + square * (
        -0.5 + square * (1.0 / 24.0 + square * (-1.0 / 720.0 + square * (1.0 / 40320.0)))
    )
    odd = (quarter & 1) == 1
    cos_value = jnp.where(odd, sine, cosine)
    sin_value = jnp.where(odd, cosine, sine)
    cos_value = jnp.where(((quarter + 1) & 2) == 2, -cos_value, cos_value)
    sin_value = jnp.where((quarter & 2) == 2, -sin_value, sin_value)
    return cos_value, sin_value


def fill_table(table, samples):
    row = lax.broadcasted_iota(jnp.int32, (16, N), 0)
    lane = lax.broadcasted_iota(jnp.int32, (16, N), 1)
    if samples:
        shift = jnp.where(row < 5, row + 6, jnp.where(row < 10, row - 4, 0))
        value = lane
    else:
        shift = jnp.where(row < 5, row + 5, jnp.where(row < 10, row - 5, 0))
        value = 2 * lane + 1
    cos_bits, sin_bits = cos_sin((value << shift) & (4 * N - 1))
    norm = math.sqrt(2.0 / N)
    if samples:
        first = jnp.where(lane[:1] == 0, math.sqrt(1.0 / N), norm)
        fine = (cos_bits[10:11] * first, sin_bits[10:11] * first)
    else:
        fine = (jnp.full((1, N), norm, F32), jnp.zeros((1, N), F32))
    table[0, 0:1], table[1, 0:1] = jnp.ones((1, N), F32), jnp.zeros((1, N), F32)
    table[2, 0:1], table[3, 0:1] = fine
    for part in range(2):
        for bit in range(5):
            at = 5 * part + bit
            size = 1 << bit
            c, s = table[2 * part, 0:size], table[2 * part + 1, 0:size]
            cb, sb = cos_bits[at : at + 1], sin_bits[at : at + 1]
            table[2 * part, size : 2 * size] = c * cb - s * sb
            table[2 * part + 1, size : 2 * size] = s * cb + c * sb


def split(x):
    high = x.astype(BF16)
    low = (x - high.astype(F32)).astype(BF16)
    return high, low


def build(table, high, low, rows, lanes, first_row=None):
    for a in range(rows.start // 32, rows.stop // 32):
        value = table[0, a : a + 1, lanes] * table[2, :, lanes]
        value -= table[1, a : a + 1, lanes] * table[3, :, lanes]
        if first_row is not None and a == 0:
            row = lax.broadcasted_iota(jnp.int32, value.shape, 0)
            value = jnp.where(row == 0, first_row, value)
        block = slice(32 * a, 32 * a + 32)
        high[block, lanes], low[block, lanes] = split(value)


WHOLE = slice(0, N)


def build_samples(table, high, low, rows=WHOLE, lanes=WHOLE):
    build(table, high, low, rows, lanes)


def build_freqs(table, high, low, rows=WHOLE, lanes=WHOLE):
    build(table, high, low, rows, lanes, math.sqrt(1.0 / N))


def start(source, target, sem):
    copy = pltpu.make_async_copy(source, target, sem)
    copy.start()
    return copy


def dot(a, b):
    return jnp.dot(a, b, preferred_element_type=F32)


def stacked_times(stack, rows, high, low, columns):
    both = dot(stack[0 : 2 * rows, :], high[:, columns])
    return both[:rows] + both[rows:] + dot(stack[0:rows, :], low[:, columns])


def matrix_times(high, low, rows, pair, width, offset=0):
    both = dot(high[rows, :], pair[:, offset : offset + 2 * width])
    return both[:, :width] + both[:, width:] + dot(low[rows, :], pair[:, offset : offset + width])


def first_kernel(
    observed, estimate, sent,
    table_v, observed_v, estimate_v, sent_v, high, low, stack, sems,
):
    copies = [
        start(observed.at[0], observed_v, sems.at[1]),
        start(estimate.at[0], estimate_v, sems.at[2]),
    ]
    fill_table(table_v, True)
    copies[0].wait()
    stack[0:R, :], stack[2 * R : 3 * R, :] = split(observed_v[...])
    copies[1].wait()
    stack[R : 2 * R, :], stack[3 * R : 4 * R, :] = split(estimate_v[...])
    out_copies = []
    for d in range(G // 2):
        columns = slice(256 * d, 256 * d + 256)
        build_samples(table_v, high, low, WHOLE, columns)
        out = stacked_times(stack, 2 * R, high, low, columns)
        for h in range(2):
            lanes = slice(128 * h, 128 * h + 128)
            e = 2 * d + h
            sent_v[e, 0] = out[:R, lanes]
            sent_v[e, 1] = out[R:, lanes]
        out_copies.append(
            start(sent_v.at[2 * d : 2 * d + 2], sent.at[2 * d : 2 * d + 2], sems.at[4 + d])
        )
    for copy in out_copies:
        copy.wait()


def left(x):
    return pltpu.roll(x, N - 1, 1)


def weight_of(plane, row, value, last):
    column = jnp.where(last, 0.0, left(value) - value)
    square = plane * plane + row * row + column * column
    return 1.0 / jnp.maximum(jnp.sqrt(square), HUBER_EDGE)


def divergence(value, ahead_plane, behind_plane, ahead_row, behind_row, w_plane, w_back, w_row, w_row_back, w_col):
    flux_col = w_col * (left(value) - value)
    total = w_back * (value - behind_plane) - w_plane * (ahead_plane - value)
    total += w_row_back * (value - behind_row) - w_row * (ahead_row - value)
    total += pltpu.roll(flux_col, 1, 1) - flux_col
    return SMOOTHING * total


def as_tile(row):
    return jnp.concatenate([row[:, 128 * i : 128 * i + 128] for i in range(8)], axis=0)


def weights_kernel(
    place, estimate, behind, ahead, spectrum,
    sent, w_all, w_back_all, strip,
    table_v, ext, ext_back, spectrum_v, sent_v, ext_w,
    high, low, stack, sems,
):
    spectrum_copy = start(spectrum.at[0], spectrum_v, sems.at[0])
    fill_table(table_v, True)
    ok_plane = jnp.where(place[0] < 15, 1.0, 0.0)
    ok_back = jnp.where(place[0] > 0, 1.0, 0.0)
    ext[8 : 8 + R, :] = estimate[0]
    ext_back[0:R, :] = behind[0]
    ext[7:8, :] = estimate[0, 0:1, :]
    ext[8 + R : 9 + R, :] = estimate[0, R - 1 : R, :]
    ext_back[R : R + 1, :] = behind[0, R - 1 : R, :]
    ext_w[7:8, :] = jnp.zeros((1, N), F32)
    last = lax.broadcasted_iota(jnp.int32, (CHUNK, N), 1) == N - 1
    for c in range(0, R, CHUNK):
        value = ext[8 + c : 8 + c + CHUNK, :]
        back = ext_back[c : c + CHUNK, :]
        w = weight_of(
            (ahead[0, c : c + CHUNK, :] - value) * ok_plane,
            ext[9 + c : 9 + c + CHUNK, :] - value,
            value,
            last,
        )
        ext_w[8 + c : 8 + c + CHUNK, :] = w
        w_all[c : c + CHUNK, :] = w
        w_back_all[c : c + CHUNK, :] = weight_of(
            (value - back) * ok_back, ext_back[1 + c : 1 + c + CHUNK, :] - back, back, last
        ) * ok_back
    for c in range(0, R, CHUNK):
        w = ext_w[8 + c : 8 + c + CHUNK, :]
        out = divergence(
            ext[8 + c : 8 + c + CHUNK, :],
            ahead[0, c : c + CHUNK, :],
            ext_back[c : c + CHUNK, :],
            ext[9 + c : 9 + c + CHUNK, :],
            ext[7 + c : 7 + c + CHUNK, :],
            w * ok_plane,
            w_back_all[c : c + CHUNK, :],
            w,
            ext_w[7 + c : 7 + c + CHUNK, :],
            jnp.where(last, 0.0, w),
        )
        stack[c : c + CHUNK, :], stack[R + c : R + c + CHUNK, :] = split(out)
    for i, rows in enumerate((
        estimate[0, 0:2, :], estimate[0, R - 2 : R, :], ahead[0, 0:1, :], ahead[0, R - 1 : R, :],
        behind[0, 0:1, :], behind[0, R - 1 : R, :], w_all[0:1, :], w_all[R - 2 : R - 1, :],
        w_back_all[0:1, :],
    )):
        at = 2 * i if i < 2 else i + 2
        strip[at : at + rows.shape[0], :] = rows
    spectrum_copy.wait()
    out_copies = []
    for d in range(G // 2):
        columns = slice(256 * d, 256 * d + 256)
        build_samples(table_v, high, low, WHOLE, columns)
        out = stacked_times(stack, R, high, low, columns)
        for h in range(2):
            e = 2 * d + h
            sent_v[e, 0] = spectrum_v[:, 128 * e : 128 * e + 128]
            sent_v[e, 1] = out[:, 128 * h : 128 * h + 128]
        out_copies.append(
            start(sent_v.at[2 * d : 2 * d + 2], sent.at[2 * d : 2 * d + 2], sems.at[1 + d])
        )
    for copy in out_copies:
        copy.wait()


def edge_kernel(
    place, from_above, from_below, strip, half_sent, sent, w_edge,
    table_v, high, low, stack, rows_v, sems,
):
    fill_table(table_v, True)
    plane, row = place[0], place[1]
    ok_plane = jnp.where(plane < 15, 1.0, 0.0)
    ok_back = jnp.where(plane > 0, 1.0, 0.0)
    ok_top = jnp.where(row > 0, 1.0, 0.0)
    inside = row < G - 1
    last = lax.broadcasted_iota(jnp.int32, (1, N), 1) == N - 1

    def line(i):
        return strip[i : i + 1, :]

    head, second, before, tail = line(0), line(1), line(2), line(3)
    top = from_above[0]
    bottom = jnp.where(inside, from_below[0], tail)
    behind_bottom = jnp.where(inside, from_below[1], line(7))
    w_top = ok_top * weight_of(
        (from_above[1] - top) * ok_plane, (head - top) * ok_top, top, last
    )
    w_tail = weight_of((line(5) - tail) * ok_plane, bottom - tail, tail, last)
    w_back_tail = ok_back * weight_of(
        (tail - line(7)) * ok_back, behind_bottom - line(7), line(7), last
    )
    w_edge[0:1, :], w_edge[1:2, :], w_edge[2:3, :] = w_top, w_tail, w_back_tail
    w_head = line(8)
    first_row = divergence(
        head, line(4), line(6), second, top,
        w_head * ok_plane, line(10), w_head, w_top, jnp.where(last, 0.0, w_head),
    )
    last_row = divergence(
        tail, line(5), line(7), bottom, before,
        w_tail * ok_plane, w_back_tail, w_tail, line(9), jnp.where(last, 0.0, w_tail),
    )
    pair = jnp.concatenate([first_row, last_row, jnp.zeros((14, N), F32)], axis=0)
    stack[0:16, :], stack[16:32, :] = split(pair)
    out_copies = []
    for d in range(G // 2):
        columns = slice(256 * d, 256 * d + 256)
        build_samples(table_v, high, low, WHOLE, columns)
        out = stacked_times(stack, 16, high, low, columns)
        for h in range(2):
            e = 2 * d + h
            rows_v[e] = out[0:8, 128 * h : 128 * h + 128]
            for i, at in enumerate((0, R - 1)):
                out_copies.append(
                    start(rows_v.at[e, i : i + 1], sent.at[e, 1, at : at + 1], sems.at[2 * e + i])
                )
    for copy in out_copies:
        copy.wait()


def forward_kernel(got, spectral, table_v, high, low, pair):
    fill_table(table_v, False)
    for d in range(G):
        rows = slice(R * d, R * d + R)
        pair[rows, 0:128], pair[rows, 256:384] = split(got[d, 0])
        pair[rows, 128:256], pair[rows, 384:512] = split(got[d, 1])
    for m in range(4):
        rows = slice(256 * m, 256 * m + 256)
        build_freqs(table_v, high, low, rows)
        spectral[rows, :] = matrix_times(high, low, rows, pair, 256)


def middle_kernel(
    got, spectral, sent, freq_v, sample_v, f_high, f_low, s_high, s_low, pair,
):
    fill_table(freq_v, False)
    fill_table(sample_v, True)
    for d in range(G):
        rows = slice(R * d, R * d + R)
        pair[rows, 0:128], pair[rows, 128:256] = split(got[d, 1])
    for m in range(4):
        rows = slice(256 * m, 256 * m + 256)
        build_freqs(freq_v, f_high, f_low, rows)
        reg = matrix_times(f_high, f_low, rows, pair, 128)
        gain = jnp.concatenate([got[2 * m, 0], got[2 * m + 1, 0]], axis=0)
        value = gain * (spectral[rows, :128] - gain * spectral[rows, 128:]) - reg
        pair[rows, 256:384], pair[rows, 512:640] = split(value)
        pair[rows, 384:512], pair[rows, 640:768] = split(gain * gain * value)
    for d in range(G):
        sent[d, R:SECOND] = jnp.zeros((8, 128), F32)
    for m in range(4):
        rows = slice(256 * m, 256 * m + 256)
        build_samples(sample_v, s_high, s_low, rows)
        out = matrix_times(s_high, s_low, rows, pair, 256, 256)
        for h in range(2):
            d = 2 * m + h
            block = out[R * h : R * h + R]
            sent[d, 0:R] = block[:, :128]
            sent[d, SECOND:] = block[:, 128:]
            if d + 1 < G:
                sent[d + 1, R : R + 1] = block[R - 1 : R, :128]
            if d > 0:
                sent[d - 1, R + 1 : R + 2] = block[0:1, :128]


def residual_kernel(got, residual, image, edges, table_v, f_high, f_low, stack):
    fill_table(table_v, False)
    rows = BOTH + 8
    pad = jnp.zeros((8, 128), BF16)
    for d in range(G):
        lanes = slice(128 * d, 128 * d + 128)
        high, low = split(got[d])
        stack[0:rows, lanes] = jnp.concatenate([high, pad], axis=0)
        stack[rows : 2 * rows, lanes] = jnp.concatenate([low, pad], axis=0)
    for d in range(G // 2):
        lanes = slice(256 * d, 256 * d + 256)
        build_freqs(table_v, f_high, f_low, WHOLE, lanes)
        out = stacked_times(stack, rows, f_high, f_low, lanes)
        residual[0, :, lanes] = out[:R]
        edges[0:2, lanes] = out[R : R + 2]
        image[:, lanes] = out[SECOND:BOTH]


def patched(weights, w_edge, c, line):
    w = weights[c : c + CHUNK, :]
    if c + CHUNK < R:
        return w
    row = lax.broadcasted_iota(jnp.int32, (CHUNK, N), 0)
    return jnp.where(row == CHUNK - 1, w_edge[line : line + 1, :], w)


def extend(place, residual, edges, ext):
    ext[7:8, :] = edges[0:1, :]
    ext[8 : 8 + R, :] = residual[0]
    ext[8 + R : 9 + R, :] = jnp.where(place[1] < G - 1, edges[1:2, :], residual[0, R - 1 : R, :])


def partial_kernel(place, residual, edges, w_all, w_edge, image, parts, ext):
    extend(place, residual, edges, ext)
    last = lax.broadcasted_iota(jnp.int32, (CHUNK, N), 1) == N - 1
    norm = jnp.zeros((8, N), F32)
    product = jnp.zeros((8, N), F32)
    for c in range(0, R, CHUNK):
        value = ext[8 + c : 8 + c + CHUNK, :]
        row = ext[9 + c : 9 + c + CHUNK, :] - value
        column = jnp.where(last, 0.0, left(value) - value)
        cross = (SMOOTHING * patched(w_all, w_edge, c, 1)) * (row * row + column * column)
        cross += value * image[c : c + CHUNK, :]
        square = value * value
        norm += square[:8] + square[8:]
        product += cross[:8] + cross[8:]
    parts[0] = norm
    parts[1] = product


def product_kernel(place, residual, ahead, w_all, w_edge, parts, sent):
    total = jnp.zeros((8, N), F32)
    for c in range(0, R, CHUNK):
        plane = ahead[0, c : c + CHUNK, :] - residual[0, c : c + CHUNK, :]
        cross = patched(w_all, w_edge, c, 1) * (plane * plane)
        total += cross[:8] + cross[8:]
    product = parts[1] + jnp.where(place[0] < 15, SMOOTHING, 0.0) * total
    norm = jnp.sum(as_tile(jnp.sum(parts[0], axis=0, keepdims=True)), axis=0, keepdims=True)
    product = jnp.sum(as_tile(jnp.sum(product, axis=0, keepdims=True)), axis=0, keepdims=True)
    lane = lax.broadcasted_iota(jnp.int32, (1, 128), 1)
    both = jnp.where(
        lane < 64, norm + pltpu.roll(norm, 64, 1), product + pltpu.roll(product, 64, 1)
    )
    sent[...] = jnp.broadcast_to(both[None], (128, 1, 128))


def inner_kernel(
    place, residual, behind, ahead, edges, w_all, w_back_all, w_edge, blurred, image, ext, ext_w,
):
    ok_plane = jnp.where(place[0] < 15, 1.0, 0.0)
    extend(place, residual, edges, ext)
    ext_w[7:8, :] = w_edge[0:1, :]
    ext_w[8 : 8 + R, :] = w_all[...]
    ext_w[7 + R : 8 + R, :] = w_edge[1:2, :]
    last = lax.broadcasted_iota(jnp.int32, (CHUNK, N), 1) == N - 1
    for c in range(0, R, CHUNK):
        w = ext_w[8 + c : 8 + c + CHUNK, :]
        image[c : c + CHUNK, :] = blurred[c : c + CHUNK, :] + divergence(
            ext[8 + c : 8 + c + CHUNK, :],
            ahead[0, c : c + CHUNK, :],
            behind[0, c : c + CHUNK, :],
            ext[9 + c : 9 + c + CHUNK, :],
            ext[7 + c : 7 + c + CHUNK, :],
            w * ok_plane,
            patched(w_back_all, w_edge, c, 2),
            w,
            ext_w[7 + c : 7 + c + CHUNK, :],
            jnp.where(last, 0.0, w),
        )


def last_kernel(
    sums, estimate, residual, image, restored, final, restored_v, final_v, sems,
):
    both = jnp.sum(sums[...], axis=0)
    lane = lax.broadcasted_iota(jnp.int32, (1, 128), 1)
    norm = jnp.sum(jnp.where(lane < 64, both, 0.0), axis=1, keepdims=True)
    product = jnp.sum(jnp.where(lane < 64, 0.0, both), axis=1, keepdims=True)
    step = norm / product
    out_copies = []
    for c in range(4):
        rows = slice(32 * c, 32 * c + 32)
        restored_v[rows] = estimate[0, rows] + step * residual[0, rows]
        out_copies.append(start(restored_v.at[rows], restored.at[0, rows], sems.at[2 * c]))
        final_v[rows] = residual[0, rows] - step * image[rows]
        out_copies.append(start(final_v.at[rows], final.at[0, rows], sems.at[2 * c + 1]))
    for copy in out_copies:
        copy.wait()


def across(x, axes):
    return lax.all_to_all(x, axes, split_axis=0, concat_axis=0, tiled=True)


def field(rows=R):
    return pltpu.VMEM((rows, N), F32)


def step(observed, estimate, spectrum):
    planes, groups = 16, G
    place = jnp.stack([lax.axis_index(PLANES), lax.axis_index(ROWS)]).astype(jnp.int32)
    up = [(i, i + 1) for i in range(planes - 1)]
    down = [(i + 1, i) for i in range(planes - 1)]
    row_up = [(i, i + 1) for i in range(groups - 1)]
    row_down = [(i + 1, i) for i in range(groups - 1)]
    big = 2 * N * N * R
    block = shape(R, N)

    behind = lax.ppermute(estimate, PLANES, up)
    ahead = lax.ppermute(estimate, PLANES, down)
    sent = call(
        first_kernel,
        (shape(G, 2, R, 128),),
        6 * big,
        (TABLE, field(), field(), pltpu.VMEM((G, 2, R, 128), F32), MATRIX, MATRIX,
         pltpu.VMEM((4 * R, N), BF16), DMA((8,))),
        (ANY,), limit=60,
    )(observed, estimate)[0]
    first = across(sent, ROWS)

    tails = jnp.concatenate([estimate[:, R - 1 :], ahead[:, R - 1 :]], axis=0)
    heads = jnp.concatenate([estimate[:, :1], behind[:, :1]], axis=0)
    from_above = lax.ppermute(tails, ROWS, row_up)
    from_below = lax.ppermute(heads, ROWS, row_down)
    half_sent, w_all, w_back, strip = call(
        weights_kernel,
        (shape(G, 2, R, 128), block, block, shape(16, N)),
        3 * big,
        (TABLE, field(R + 16), field(R + 8), field(), pltpu.VMEM((G, 2, R, 128), F32),
         field(R + 16), MATRIX, MATRIX, pltpu.VMEM((2 * R, N), BF16), DMA((5,))),
        (ANY, VMEM, VMEM, VMEM), direct=4,
    )(place, estimate, behind, ahead, spectrum)
    sent, w_edge = call(
        edge_kernel,
        (shape(G, 2, R, 128), shape(8, N)),
        big,
        (TABLE, MATRIX, MATRIX, pltpu.VMEM((32, N), BF16), pltpu.VMEM((G, 8, 128), F32),
         DMA((16,))),
        (ANY, VMEM), {4: 0}, direct=4,
    )(place, from_above, from_below, strip, half_sent)
    second = across(sent, ROWS)
    spectral = call(
        forward_kernel,
        (shape(N, 256),),
        6 * big,
        (TABLE, MATRIX, MATRIX, pltpu.VMEM((N, 512), BF16)),
        direct=9,
    )(first)[0]
    sent = call(
        middle_kernel,
        (shape(G, BOTH, 128),),
        9 * big,
        (TABLE, TABLE, MATRIX, MATRIX, MATRIX, MATRIX, pltpu.VMEM((N, 768), BF16)),
        direct=9,
    )(second, spectral)[0]
    third = across(sent, ROWS)

    residual, blurred, edges = call(
        residual_kernel,
        (shape(1, R, N), block, shape(8, N)),
        6 * big,
        (TABLE, MATRIX, MATRIX, pltpu.VMEM((2 * BOTH + 16, N), BF16)),
        direct=9,
    )(third)
    ahead = lax.ppermute(residual, PLANES, down)
    parts = call(
        partial_kernel, (shape(2, 8, N),), big // 16, (field(R + 16),), direct=9
    )(place, residual, edges, w_all, w_edge, blurred)[0]
    late, _ = lax.optimization_barrier((residual, ahead))
    behind = lax.ppermute(late, PLANES, up)
    sent = call(
        product_kernel, (shape(128, 1, 128),), big // 64, direct=9
    )(place, residual, ahead, w_all, w_edge, parts)[0]
    sums = across(sent, ALL)
    image = call(
        inner_kernel, (block,), big // 16, (field(R + 16), field(R + 16)), direct=9
    )(place, residual, behind, ahead, edges, w_all, w_back, w_edge, blurred)[0]
    return call(
        last_kernel,
        (shape(1, R, N), shape(1, R, N)),
        R * N * 4,
        (field(), field(), DMA((8,))),
        (ANY, ANY),
        direct=9,
    )(sums, estimate, residual, image)


def solution(mesh):
    finer = Mesh(
        mesh.devices.reshape(4, 2, 2, 2, 4),
        ("planes_0", "planes_1", "planes_2", "rows_0", "rows_1"),
    )
    spec = P(PLANES, ROWS, None)
    return jax.shard_map(
        step,
        mesh=finer,
        in_specs=(spec, spec, spec),
        out_specs=(spec, spec),
        check_vma=False,
    )
```

```python
import math

import jax
import jax.numpy as jnp
from jax import lax
from jax.experimental import pallas as pl
from jax.experimental.pallas import tpu as pltpu
from jax.sharding import Mesh
from jax.sharding import PartitionSpec as P


PLANES = ("planes_0", "planes_1", "planes_2")
ROWS = ("rows_0", "rows_1")
N = 1024
R = 128
G = 8
EDGE = R + 8
REG = R + 16
FULL = 2 * R + 16
HUBER_EDGE = 0.5
SMOOTHING = 0.3
F32 = jnp.float32
BF16 = jnp.bfloat16
VMEM = pl.BlockSpec(memory_space=pltpu.VMEM)
SMEM = pl.BlockSpec(memory_space=pltpu.SMEM)
ANY = pl.BlockSpec(memory_space=pl.ANY)
HBM = pl.BlockSpec(memory_space=pltpu.HBM)
DMA = pltpu.SemaphoreType.DMA
TABLE = pltpu.VMEM((4, 32, N), F32)
MATRIX = pltpu.VMEM((N, N), BF16)
CHUNK = 16


def shape(*dims, dtype=F32):
    return jax.ShapeDtypeStruct(dims, dtype)


def call(body, outs, flops, scratch=(), out_specs=None, aliases=None, limit=32, direct=0):
    def place_of(i, a):
        if a.dtype == jnp.int32:
            return SMEM
        return VMEM if i < direct else ANY

    def launch(*args):
        size = sum(math.prod(a.shape) * a.dtype.itemsize for a in args)
        size += sum(math.prod(o.shape) * o.dtype.itemsize for o in outs)
        return pl.pallas_call(
            body,
            out_shape=tuple(outs),
            in_specs=[place_of(i, a) for i, a in enumerate(args)],
            out_specs=out_specs or tuple(VMEM for _ in outs),
            scratch_shapes=list(scratch),
            input_output_aliases=aliases or {},
            compiler_params=pltpu.CompilerParams(vmem_limit_bytes=limit << 20),
            cost_estimate=pl.CostEstimate(flops=flops, bytes_accessed=size, transcendentals=0),
        )(*args)

    return launch


def cos_sin(units):
    quarter = (units + 512) >> 10
    angle = (units - (quarter << 10)).astype(F32) * (math.pi / (2.0 * N))
    square = angle * angle
    sine = angle * (
        1.0 + square * (-1.0 / 6.0 + square * (1.0 / 120.0 + square * (-1.0 / 5040.0)))
    )
    cosine = 1.0 + square * (
        -0.5 + square * (1.0 / 24.0 + square * (-1.0 / 720.0 + square * (1.0 / 40320.0)))
    )
    odd = (quarter & 1) == 1
    cos_value = jnp.where(odd, sine, cosine)
    sin_value = jnp.where(odd, cosine, sine)
    cos_value = jnp.where(((quarter + 1) & 2) == 2, -cos_value, cos_value)
    sin_value = jnp.where((quarter & 2) == 2, -sin_value, sin_value)
    return cos_value, sin_value


def fill_table(table, samples):
    row = lax.broadcasted_iota(jnp.int32, (16, N), 0)
    lane = lax.broadcasted_iota(jnp.int32, (16, N), 1)
    if samples:
        shift = jnp.where(row < 5, row + 6, jnp.where(row < 10, row - 4, 0))
        value = lane
    else:
        shift = jnp.where(row < 5, row + 5, jnp.where(row < 10, row - 5, 0))
        value = 2 * lane + 1
    cos_bits, sin_bits = cos_sin((value << shift) & (4 * N - 1))
    norm = math.sqrt(2.0 / N)
    if samples:
        first = jnp.where(lane[:1] == 0, math.sqrt(1.0 / N), norm)
        fine = (cos_bits[10:11] * first, sin_bits[10:11] * first)
    else:
        fine = (jnp.full((1, N), norm, F32), jnp.zeros((1, N), F32))
    table[0, 0:1], table[1, 0:1] = jnp.ones((1, N), F32), jnp.zeros((1, N), F32)
    table[2, 0:1], table[3, 0:1] = fine
    for part in range(2):
        for bit in range(5):
            at = 5 * part + bit
            size = 1 << bit
            c, s = table[2 * part, 0:size], table[2 * part + 1, 0:size]
            cb, sb = cos_bits[at : at + 1], sin_bits[at : at + 1]
            table[2 * part, size : 2 * size] = c * cb - s * sb
            table[2 * part + 1, size : 2 * size] = s * cb + c * sb


def split(x):
    high = x.astype(BF16)
    low = (x - high.astype(F32)).astype(BF16)
    return high, low


def build(table, high, low, rows, lanes, first_row=None):
    for a in range(rows.start // 32, rows.stop // 32):
        value = table[0, a : a + 1, lanes] * table[2, :, lanes]
        value -= table[1, a : a + 1, lanes] * table[3, :, lanes]
        if first_row is not None and a == 0:
            row = lax.broadcasted_iota(jnp.int32, value.shape, 0)
            value = jnp.where(row == 0, first_row, value)
        block = slice(32 * a, 32 * a + 32)
        high[block, lanes], low[block, lanes] = split(value)


WHOLE = slice(0, N)


def build_samples(table, high, low, rows=WHOLE, lanes=WHOLE):
    build(table, high, low, rows, lanes)


def build_freqs(table, high, low, rows=WHOLE, lanes=WHOLE):
    build(table, high, low, rows, lanes, math.sqrt(1.0 / N))


def start(source, target, sem):
    copy = pltpu.make_async_copy(source, target, sem)
    copy.start()
    return copy


def dot(a, b):
    return jnp.dot(a, b, preferred_element_type=F32)


def stacked_times(stack, rows, high, low, columns):
    both = dot(stack[0 : 2 * rows, :], high[:, columns])
    return both[:rows] + both[rows:] + dot(stack[0:rows, :], low[:, columns])


def matrix_times(high, low, rows, pair, width, offset=0):
    both = dot(high[rows, :], pair[:, offset : offset + 2 * width])
    return both[:, :width] + both[:, width:] + dot(low[rows, :], pair[:, offset : offset + width])


def first_kernel(
    observed, estimate, spectrum, sent,
    table_v, observed_v, estimate_v, spectrum_v, sent_v, high, low, stack, sems,
):
    copies = [
        start(observed.at[0], observed_v, sems.at[1]),
        start(estimate.at[0], estimate_v, sems.at[2]),
        start(spectrum.at[0], spectrum_v, sems.at[3]),
    ]
    fill_table(table_v, True)
    copies[0].wait()
    stack[0:R, :], stack[2 * R : 3 * R, :] = split(observed_v[...])
    copies[1].wait()
    stack[R : 2 * R, :], stack[3 * R : 4 * R, :] = split(estimate_v[...])
    copies[2].wait()
    out_copies = []
    for d in range(G // 2):
        columns = slice(256 * d, 256 * d + 256)
        build_samples(table_v, high, low, WHOLE, columns)
        out = stacked_times(stack, 2 * R, high, low, columns)
        for h in range(2):
            lanes = slice(128 * h, 128 * h + 128)
            e = 2 * d + h
            sent_v[e, 0] = out[:R, lanes]
            sent_v[e, 1] = out[R:, lanes]
            sent_v[e, 2] = spectrum_v[:, 128 * e : 128 * e + 128]
        out_copies.append(
            start(sent_v.at[2 * d : 2 * d + 2], sent.at[2 * d : 2 * d + 2], sems.at[4 + d])
        )
    for copy in out_copies:
        copy.wait()


def left(x):
    return pltpu.roll(x, N - 1, 1)


def weight_of(plane, row, value, last):
    column = jnp.where(last, 0.0, left(value) - value)
    square = plane * plane + row * row + column * column
    return 1.0 / jnp.maximum(jnp.sqrt(square), HUBER_EDGE)


def divergence(value, ahead_plane, behind_plane, ahead_row, behind_row, w_plane, w_back, w_row, w_row_back, w_col):
    flux_col = w_col * (left(value) - value)
    total = w_back * (value - behind_plane) - w_plane * (ahead_plane - value)
    total += w_row_back * (value - behind_row) - w_row * (ahead_row - value)
    total += pltpu.roll(flux_col, 1, 1) - flux_col
    return SMOOTHING * total


def as_tile(row):
    return jnp.concatenate([row[:, 128 * i : 128 * i + 128] for i in range(8)], axis=0)


def weights_kernel(
    place, estimate, behind, ahead,
    sent, reg, w_all, w_back_all, strip,
    table_v, ext, ext_back, sent_v, ext_w,
    high, low, stack, sems,
):
    fill_table(table_v, True)
    ok_plane = jnp.where(place[0] < 15, 1.0, 0.0)
    ok_back = jnp.where(place[0] > 0, 1.0, 0.0)
    ext[8 : 8 + R, :] = estimate[0]
    ext_back[0:R, :] = behind[0]
    ext[7:8, :] = estimate[0, 0:1, :]
    ext[8 + R : 9 + R, :] = estimate[0, R - 1 : R, :]
    ext_back[R : R + 1, :] = behind[0, R - 1 : R, :]
    ext_w[7:8, :] = jnp.zeros((1, N), F32)
    last = lax.broadcasted_iota(jnp.int32, (CHUNK, N), 1) == N - 1
    for c in range(0, R, CHUNK):
        value = ext[8 + c : 8 + c + CHUNK, :]
        back = ext_back[c : c + CHUNK, :]
        w = weight_of(
            (ahead[0, c : c + CHUNK, :] - value) * ok_plane,
            ext[9 + c : 9 + c + CHUNK, :] - value,
            value,
            last,
        )
        ext_w[8 + c : 8 + c + CHUNK, :] = w
        w_all[c : c + CHUNK, :] = w
        w_back_all[c : c + CHUNK, :] = weight_of(
            (value - back) * ok_back, ext_back[1 + c : 1 + c + CHUNK, :] - back, back, last
        ) * ok_back
    for c in range(0, R, CHUNK):
        w = ext_w[8 + c : 8 + c + CHUNK, :]
        out = divergence(
            ext[8 + c : 8 + c + CHUNK, :],
            ahead[0, c : c + CHUNK, :],
            ext_back[c : c + CHUNK, :],
            ext[9 + c : 9 + c + CHUNK, :],
            ext[7 + c : 7 + c + CHUNK, :],
            w * ok_plane,
            w_back_all[c : c + CHUNK, :],
            w,
            ext_w[7 + c : 7 + c + CHUNK, :],
            jnp.where(last, 0.0, w),
        )
        reg[c : c + CHUNK, :] = out
        stack[c : c + CHUNK, :], stack[R + c : R + c + CHUNK, :] = split(out)
    for i, rows in enumerate((
        estimate[0, 0:2, :], estimate[0, R - 2 : R, :], ahead[0, 0:1, :], ahead[0, R - 1 : R, :],
        behind[0, 0:1, :], behind[0, R - 1 : R, :], w_all[0:1, :], w_all[R - 2 : R - 1, :],
        w_back_all[0:1, :],
    )):
        at = 2 * i if i < 2 else i + 2
        strip[at : at + rows.shape[0], :] = rows
    out_copies = []
    for d in range(G // 2):
        columns = slice(256 * d, 256 * d + 256)
        build_samples(table_v, high, low, WHOLE, columns)
        out = stacked_times(stack, R, high, low, columns)
        for h in range(2):
            e = 2 * d + h
            sent_v[e] = out[:, 128 * h : 128 * h + 128]
        out_copies.append(
            start(sent_v.at[2 * d : 2 * d + 2], sent.at[2 * d : 2 * d + 2, REG:], sems.at[1 + d])
        )
    for copy in out_copies:
        copy.wait()


def edge_kernel(
    place, from_above, from_below, strip, half_sent, sent, w_edge,
    table_v, high, low, stack, rows_v, tiles_v, sems,
):
    fill_table(table_v, True)
    plane, row = place[0], place[1]
    ok_plane = jnp.where(plane < 15, 1.0, 0.0)
    ok_back = jnp.where(plane > 0, 1.0, 0.0)
    ok_top = jnp.where(row > 0, 1.0, 0.0)
    inside = row < G - 1
    last = lax.broadcasted_iota(jnp.int32, (1, N), 1) == N - 1

    def line(i):
        return strip[i : i + 1, :]

    head, second, before, tail = line(0), line(1), line(2), line(3)
    top = from_above[0]
    bottom = jnp.where(inside, from_below[0], tail)
    behind_bottom = jnp.where(inside, from_below[1], line(7))
    w_top = ok_top * weight_of(
        (from_above[1] - top) * ok_plane, (head - top) * ok_top, top, last
    )
    w_tail = weight_of((line(5) - tail) * ok_plane, bottom - tail, tail, last)
    w_back_tail = ok_back * weight_of(
        (tail - line(7)) * ok_back, behind_bottom - line(7), line(7), last
    )
    w_edge[0:1, :], w_edge[1:2, :], w_edge[2:3, :] = w_top, w_tail, w_back_tail
    w_head = line(8)
    first_row = divergence(
        head, line(4), line(6), second, top,
        w_head * ok_plane, line(10), w_head, w_top, jnp.where(last, 0.0, w_head),
    )
    last_row = divergence(
        tail, line(5), line(7), bottom, before,
        w_tail * ok_plane, w_back_tail, w_tail, line(9), jnp.where(last, 0.0, w_tail),
    )
    w_edge[3:4, :], w_edge[4:5, :] = first_row, last_row
    head_tile, tail_tile = as_tile(first_row), as_tile(last_row)
    for e in range(G):
        tiles_v[e] = jnp.where(row == e - 1, tail_tile, jnp.where(row == e + 1, head_tile, 0.0))
    tile_copy = start(tiles_v, sent.at[:, EDGE:REG], sems.at[16])
    pair = jnp.concatenate([first_row, last_row, jnp.zeros((14, N), F32)], axis=0)
    stack[0:16, :], stack[16:32, :] = split(pair)
    out_copies = []
    for d in range(G // 2):
        columns = slice(256 * d, 256 * d + 256)
        build_samples(table_v, high, low, WHOLE, columns)
        out = stacked_times(stack, 16, high, low, columns)
        for h in range(2):
            e = 2 * d + h
            rows_v[e] = out[0:8, 128 * h : 128 * h + 128]
            for i, at in enumerate((0, R - 1)):
                out_copies.append(
                    start(rows_v.at[e, i : i + 1], sent.at[e, REG + at : REG + at + 1], sems.at[2 * e + i])
                )
    tile_copy.wait()
    for copy in out_copies:
        copy.wait()


def middle_kernel(
    got, half_sent, sent, spectral, freq_v, sample_v, sent_v, f_high, f_low, s_high, s_low, pair,
    sems,
):
    fill_table(freq_v, False)
    fill_table(sample_v, True)
    for d in range(G):
        rows = slice(R * d, R * d + R)
        pair[rows, 0:128], pair[rows, 256:384] = split(got[d, 0])
        pair[rows, 128:256], pair[rows, 384:512] = split(got[d, 1])
        sent_v[d, R:] = jnp.zeros((8, 128), F32)
    for m in range(4):
        rows = slice(256 * m, 256 * m + 256)
        build_freqs(freq_v, f_high, f_low, rows)
        out = matrix_times(f_high, f_low, rows, pair, 256)
        gain = jnp.concatenate([got[2 * m, 2], got[2 * m + 1, 2]], axis=0)
        value = gain * (out[:, :128] - gain * out[:, 128:])
        spectral[rows, :128] = value
        spectral[rows, 128:] = gain
        pair[rows, 512:640], pair[rows, 640:768] = split(value)
    out_copies = []
    for m in range(4):
        rows = slice(256 * m, 256 * m + 256)
        build_samples(sample_v, s_high, s_low, rows)
        out = matrix_times(s_high, s_low, rows, pair, 128, 512)
        for h in range(2):
            d = 2 * m + h
            block = out[R * h : R * h + R]
            sent_v[d, 0:R] = block
            if d + 1 < G:
                sent_v[d + 1, R : R + 1] = block[R - 1 : R]
            if d > 0:
                sent_v[d - 1, R + 1 : R + 2] = block[0:1]
                out_copies.append(start(sent_v.at[d - 1], sent.at[d - 1, 0:EDGE], sems.at[d]))
    out_copies.append(start(sent_v.at[G - 1], sent.at[G - 1, 0:EDGE], sems.at[0]))
    for copy in out_copies:
        copy.wait()


def residual_kernel(
    place, got, reg, w_edge, residual, edges, table_v, rows_v, f_high, f_low, stack,
):
    row = place[1]
    fill_table(table_v, False)
    above = got[jnp.maximum(row - 1, 0), EDGE:REG, :]
    below = got[jnp.minimum(row + 1, G - 1), EDGE:REG, :]
    for i in range(G):
        rows_v[0:1, 128 * i : 128 * i + 128] = above[i : i + 1]
        rows_v[1:2, 128 * i : 128 * i + 128] = below[i : i + 1]
    rows = R + 16
    for d in range(G):
        lanes = slice(128 * d, 128 * d + 128)
        stack[0:rows, lanes], stack[rows : 2 * rows, lanes] = split(got[d, 0:rows])
    for d in range(G // 2):
        lanes = slice(256 * d, 256 * d + 256)
        build_freqs(table_v, f_high, f_low, WHOLE, lanes)
        out = stacked_times(stack, rows, f_high, f_low, lanes)
        residual[0, :, lanes] = out[:R] - reg[:, lanes]
        residual[0, 0:1, lanes] = out[0:1] - w_edge[3:4, lanes]
        residual[0, R - 1 : R, lanes] = out[R - 1 : R] - w_edge[4:5, lanes]
        edges[0:2, lanes] = out[R : R + 2] - rows_v[0:2, lanes]


def curvature_kernel(
    got, spectral, sent, total, freq_v, sample_v, sent_v, f_high, f_low, s_high, s_low, pair, sems,
):
    fill_table(freq_v, False)
    fill_table(sample_v, True)
    for d in range(G):
        rows = slice(R * d, R * d + R)
        pair[rows, 0:128], pair[rows, 128:256] = split(got[d, REG:])
    acc = jnp.zeros((8, 128), F32)
    for m in range(4):
        rows = slice(256 * m, 256 * m + 256)
        build_freqs(freq_v, f_high, f_low, rows)
        out = spectral[rows, :128] - matrix_times(f_high, f_low, rows, pair, 128)
        gain = spectral[rows, 128:]
        scaled = gain * gain * out
        acc += jnp.sum((scaled * out).reshape(32, 8, 128), axis=0)
        pair[rows, 256:384], pair[rows, 384:512] = split(scaled)
    total[...] = acc
    out_copies = []
    for m in range(4):
        rows = slice(256 * m, 256 * m + 256)
        build_samples(sample_v, s_high, s_low, rows)
        out = matrix_times(s_high, s_low, rows, pair, 128, 256)
        sent_v[2 * m] = out[:R]
        sent_v[2 * m + 1] = out[R:]
        out_copies.append(
            start(sent_v.at[2 * m : 2 * m + 2], sent.at[2 * m : 2 * m + 2, 0:R], sems.at[m])
        )
    for copy in out_copies:
        copy.wait()


def patched(weights, w_edge, c, line):
    w = weights[c : c + CHUNK, :]
    if c + CHUNK < R:
        return w
    row = lax.broadcasted_iota(jnp.int32, (CHUNK, N), 0)
    return jnp.where(row == CHUNK - 1, w_edge[line : line + 1, :], w)


def extend(place, residual, edges, ext):
    ext[7:8, :] = edges[0:1, :]
    ext[8 : 8 + R, :] = residual[0]
    ext[8 + R : 9 + R, :] = jnp.where(place[1] < G - 1, edges[1:2, :], residual[0, R - 1 : R, :])


def partial_kernel(place, residual, edges, w_all, w_edge, parts, ext):
    extend(place, residual, edges, ext)
    last = lax.broadcasted_iota(jnp.int32, (CHUNK, N), 1) == N - 1
    norm = jnp.zeros((8, N), F32)
    product = jnp.zeros((8, N), F32)
    for c in range(0, R, CHUNK):
        value = ext[8 + c : 8 + c + CHUNK, :]
        row = ext[9 + c : 9 + c + CHUNK, :] - value
        column = jnp.where(last, 0.0, left(value) - value)
        cross = (SMOOTHING * patched(w_all, w_edge, c, 1)) * (row * row + column * column)
        square = value * value
        norm += square[:8] + square[8:]
        product += cross[:8] + cross[8:]
    parts[0] = norm
    parts[1] = product


def product_kernel(
    place, residual, ahead, w_all, w_edge, parts, total, half, sent, tile_v, sems,
):
    acc = jnp.zeros((8, N), F32)
    for c in range(0, R, CHUNK):
        plane = ahead[0, c : c + CHUNK, :] - residual[0, c : c + CHUNK, :]
        cross = patched(w_all, w_edge, c, 1) * (plane * plane)
        acc += cross[:8] + cross[8:]
    product = parts[1] + jnp.where(place[0] < 15, SMOOTHING, 0.0) * acc
    norm = jnp.sum(as_tile(jnp.sum(parts[0], axis=0, keepdims=True)), axis=0, keepdims=True)
    product = as_tile(jnp.sum(product, axis=0, keepdims=True)) + total[...]
    product = jnp.sum(product, axis=0, keepdims=True)
    tile_v[...] = jnp.concatenate([norm, product, jnp.zeros((6, 128), F32)], axis=0)
    out_copies = [start(tile_v, sent.at[d, R:], sems.at[d]) for d in range(G)]
    for copy in out_copies:
        copy.wait()


def inner_kernel(
    place, residual, behind, ahead, edges, w_all, w_back_all, w_edge, image, ext, ext_w,
):
    ok_plane = jnp.where(place[0] < 15, 1.0, 0.0)
    extend(place, residual, edges, ext)
    ext_w[7:8, :] = w_edge[0:1, :]
    ext_w[8 : 8 + R, :] = w_all[...]
    ext_w[7 + R : 8 + R, :] = w_edge[1:2, :]
    last = lax.broadcasted_iota(jnp.int32, (CHUNK, N), 1) == N - 1
    for c in range(0, R, CHUNK):
        w = ext_w[8 + c : 8 + c + CHUNK, :]
        image[c : c + CHUNK, :] = divergence(
            ext[8 + c : 8 + c + CHUNK, :],
            ahead[0, c : c + CHUNK, :],
            behind[0, c : c + CHUNK, :],
            ext[9 + c : 9 + c + CHUNK, :],
            ext[7 + c : 7 + c + CHUNK, :],
            w * ok_plane,
            patched(w_back_all, w_edge, c, 2),
            w,
            ext_w[7 + c : 7 + c + CHUNK, :],
            jnp.where(last, 0.0, w),
        )


def last_kernel(
    sums, got, reg, residual, estimate, restored, final,
    table_v, restored_v, final_v, f_high, f_low, stack, sems,
):
    fill_table(table_v, False)
    for d in range(G):
        lanes = slice(128 * d, 128 * d + 128)
        stack[0:R, lanes], stack[R : 2 * R, lanes] = split(got[d, 0:R])
    tile = jnp.sum(sums[...], axis=0)
    norm = jnp.sum(tile[0:1, :], axis=1, keepdims=True)
    product = jnp.sum(tile[1:2, :], axis=1, keepdims=True)
    step = norm / product
    restored_v[...] = estimate[0] + step * residual[0]
    out_copies = [start(restored_v, restored.at[0], sems.at[4])]
    for d in range(G // 2):
        lanes = slice(256 * d, 256 * d + 256)
        build_freqs(table_v, f_high, f_low, WHOLE, lanes)
        image = stacked_times(stack, R, f_high, f_low, lanes) + reg[:, lanes]
        final_v[:, lanes] = residual[0, :, lanes] - step * image
        out_copies.append(start(final_v.at[:, lanes], final.at[0, :, lanes], sems.at[d]))
    for copy in out_copies:
        copy.wait()


def across(x, axes):
    return lax.all_to_all(x, axes, split_axis=0, concat_axis=0, tiled=True)


def field(rows=R):
    return pltpu.VMEM((rows, N), F32)


def step(observed, estimate, spectrum):
    planes, groups = 16, G
    place = jnp.stack([lax.axis_index(PLANES), lax.axis_index(ROWS)]).astype(jnp.int32)
    up = [(i, i + 1) for i in range(planes - 1)]
    down = [(i + 1, i) for i in range(planes - 1)]
    row_up = [(i, i + 1) for i in range(groups - 1)]
    row_down = [(i + 1, i) for i in range(groups - 1)]
    big = 2 * N * N * R
    block = shape(R, N)

    behind = lax.ppermute(estimate, PLANES, up)
    ahead = lax.ppermute(estimate, PLANES, down)
    sent = call(
        first_kernel,
        (shape(G, 3, R, 128),),
        6 * big,
        (TABLE, field(), field(), field(), pltpu.VMEM((G, 3, R, 128), F32), MATRIX, MATRIX,
         pltpu.VMEM((4 * R, N), BF16), DMA((8,))),
        (ANY,), limit=60,
    )(observed, estimate, spectrum)[0]
    first = across(sent, ROWS)

    tails = jnp.concatenate([estimate[:, R - 1 :], ahead[:, R - 1 :]], axis=0)
    heads = jnp.concatenate([estimate[:, :1], behind[:, :1]], axis=0)
    from_above = lax.ppermute(tails, ROWS, row_up)
    from_below = lax.ppermute(heads, ROWS, row_down)
    wide = shape(G, FULL, 128)
    half_sent, reg, w_all, w_back, strip = call(
        weights_kernel,
        (wide, block, block, block, shape(16, N)),
        3 * big,
        (TABLE, field(R + 16), field(R + 8), pltpu.VMEM((G, R, 128), F32),
         field(R + 16), MATRIX, MATRIX, pltpu.VMEM((2 * R, N), BF16), DMA((5,))),
        (ANY, VMEM, VMEM, VMEM, VMEM), direct=4,
    )(place, estimate, behind, ahead)
    half_sent, w_edge = call(
        edge_kernel,
        (wide, shape(8, N)),
        big,
        (TABLE, MATRIX, MATRIX, pltpu.VMEM((32, N), BF16), pltpu.VMEM((G, 8, 128), F32),
         pltpu.VMEM((G, 8, 128), F32), DMA((17,))),
        (ANY, VMEM), {4: 0}, direct=4,
    )(place, from_above, from_below, strip, half_sent)
    sent, spectral = call(
        middle_kernel,
        (wide, shape(N, 256)),
        9 * big,
        (TABLE, TABLE, pltpu.VMEM((G, EDGE, 128), F32), MATRIX, MATRIX, MATRIX, MATRIX,
         pltpu.VMEM((N, 768), BF16), DMA((8,))),
        (ANY, VMEM), {1: 0}, direct=1,
    )(first, half_sent)
    second = across(sent, ROWS)

    residual, edges = call(
        residual_kernel,
        (shape(1, R, N), shape(8, N)),
        3 * big,
        (TABLE, field(8), MATRIX, MATRIX, pltpu.VMEM((2 * R + 32, N), BF16)),
        direct=9,
    )(place, second, reg, w_edge)
    ahead = lax.ppermute(residual, PLANES, down)
    parts = call(
        partial_kernel, (shape(2, 8, N),), big // 16, (field(R + 16),), direct=9
    )(place, residual, edges, w_all, w_edge)[0]
    half_sent, total = call(
        curvature_kernel,
        (shape(G, EDGE, 128), shape(8, 128)),
        6 * big,
        (TABLE, TABLE, pltpu.VMEM((G, R, 128), F32), MATRIX, MATRIX, MATRIX, MATRIX,
         pltpu.VMEM((N, 512), BF16), DMA((4,))),
        (ANY, VMEM), direct=2,
    )(second, spectral)
    late, _ = lax.optimization_barrier((residual, ahead))
    behind = lax.ppermute(late, PLANES, up)
    sent = call(
        product_kernel,
        (shape(G, EDGE, 128),),
        big // 64,
        (pltpu.VMEM((8, 128), F32), DMA((8,))),
        (ANY,), {7: 0}, direct=7,
    )(place, residual, ahead, w_all, w_edge, parts, total, half_sent)[0]
    third = across(sent, ROWS)
    reg_residual = call(
        inner_kernel, (block,), big // 16, (field(R + 16), field(R + 16)), direct=9
    )(place, residual, behind, ahead, edges, w_all, w_back, w_edge)[0]
    tile = jnp.sum(third[:, R:], axis=0)
    sums = across(jnp.broadcast_to(tile[None], (planes, 8, 128)), PLANES)
    return call(
        last_kernel,
        (shape(1, R, N), shape(1, R, N)),
        3 * big,
        (TABLE, field(), field(), MATRIX, MATRIX, pltpu.VMEM((2 * R, N), BF16), DMA((5,))),
        (ANY, ANY), direct=9,
    )(sums, third, reg_residual, residual, estimate)


def solution(mesh):
    finer = Mesh(
        mesh.devices.reshape(4, 2, 2, 2, 4),
        ("planes_0", "planes_1", "planes_2", "rows_0", "rows_1"),
    )
    spec = P(PLANES, ROWS, None)
    return jax.shard_map(
        step,
        mesh=finer,
        in_specs=(spec, spec, spec),
        out_specs=(spec, spec),
        check_vma=False,
    )
```

```python
import math

import jax
import jax.numpy as jnp
from jax import lax
from jax.experimental import pallas as pl
from jax.experimental.pallas import tpu as pltpu
from jax.sharding import Mesh
from jax.sharding import PartitionSpec as P


PLANES = ("planes_0", "planes_1", "planes_2")
ROWS = ("rows_0", "rows_1")
N = 1024
R = 128
G = 8
EDGE = R + 8
REG = R + 16
FULL = 2 * R + 16
HUBER_EDGE = 0.5
SMOOTHING = 0.3
F32 = jnp.float32
BF16 = jnp.bfloat16
VMEM = pl.BlockSpec(memory_space=pltpu.VMEM)
SMEM = pl.BlockSpec(memory_space=pltpu.SMEM)
ANY = pl.BlockSpec(memory_space=pl.ANY)
HBM = pl.BlockSpec(memory_space=pltpu.HBM)
DMA = pltpu.SemaphoreType.DMA
TABLE = pltpu.VMEM((4, 32, N), F32)
MATRIX = pltpu.VMEM((N, N), BF16)
CHUNK = 16


def shape(*dims, dtype=F32):
    return jax.ShapeDtypeStruct(dims, dtype)


def call(body, outs, flops, scratch=(), out_specs=None, aliases=None, limit=32, direct=0):
    def place_of(i, a):
        if a.dtype == jnp.int32:
            return SMEM
        return VMEM if i < direct else ANY

    def launch(*args):
        size = sum(math.prod(a.shape) * a.dtype.itemsize for a in args)
        size += sum(math.prod(o.shape) * o.dtype.itemsize for o in outs)
        return pl.pallas_call(
            body,
            out_shape=tuple(outs),
            in_specs=[place_of(i, a) for i, a in enumerate(args)],
            out_specs=out_specs or tuple(VMEM for _ in outs),
            scratch_shapes=list(scratch),
            input_output_aliases=aliases or {},
            compiler_params=pltpu.CompilerParams(vmem_limit_bytes=limit << 20),
            cost_estimate=pl.CostEstimate(flops=flops, bytes_accessed=size, transcendentals=0),
        )(*args)

    return launch


def cos_sin(units):
    quarter = (units + 512) >> 10
    angle = (units - (quarter << 10)).astype(F32) * (math.pi / (2.0 * N))
    square = angle * angle
    sine = angle * (
        1.0 + square * (-1.0 / 6.0 + square * (1.0 / 120.0 + square * (-1.0 / 5040.0)))
    )
    cosine = 1.0 + square * (
        -0.5 + square * (1.0 / 24.0 + square * (-1.0 / 720.0 + square * (1.0 / 40320.0)))
    )
    odd = (quarter & 1) == 1
    cos_value = jnp.where(odd, sine, cosine)
    sin_value = jnp.where(odd, cosine, sine)
    cos_value = jnp.where(((quarter + 1) & 2) == 2, -cos_value, cos_value)
    sin_value = jnp.where((quarter & 2) == 2, -sin_value, sin_value)
    return cos_value, sin_value


def fill_table(table, samples):
    row = lax.broadcasted_iota(jnp.int32, (16, N), 0)
    lane = lax.broadcasted_iota(jnp.int32, (16, N), 1)
    if samples:
        shift = jnp.where(row < 5, row + 6, jnp.where(row < 10, row - 4, 0))
        value = lane
    else:
        shift = jnp.where(row < 5, row + 5, jnp.where(row < 10, row - 5, 0))
        value = 2 * lane + 1
    cos_bits, sin_bits = cos_sin((value << shift) & (4 * N - 1))
    norm = math.sqrt(2.0 / N)
    if samples:
        first = jnp.where(lane[:1] == 0, math.sqrt(1.0 / N), norm)
        fine = (cos_bits[10:11] * first, sin_bits[10:11] * first)
    else:
        fine = (jnp.full((1, N), norm, F32), jnp.zeros((1, N), F32))
    table[0, 0:1], table[1, 0:1] = jnp.ones((1, N), F32), jnp.zeros((1, N), F32)
    table[2, 0:1], table[3, 0:1] = fine
    for part in range(2):
        for bit in range(5):
            at = 5 * part + bit
            size = 1 << bit
            c, s = table[2 * part, 0:size], table[2 * part + 1, 0:size]
            cb, sb = cos_bits[at : at + 1], sin_bits[at : at + 1]
            table[2 * part, size : 2 * size] = c * cb - s * sb
            table[2 * part + 1, size : 2 * size] = s * cb + c * sb


def split(x):
    high = x.astype(BF16)
    low = (x - high.astype(F32)).astype(BF16)
    return high, low


def build(table, high, low, rows, lanes, first_row=None):
    for a in range(rows.start // 32, rows.stop // 32):
        value = table[0, a : a + 1, lanes] * table[2, :, lanes]
        value -= table[1, a : a + 1, lanes] * table[3, :, lanes]
        if first_row is not None and a == 0:
            row = lax.broadcasted_iota(jnp.int32, value.shape, 0)
            value = jnp.where(row == 0, first_row, value)
        block = slice(32 * a, 32 * a + 32)
        high[block, lanes], low[block, lanes] = split(value)


WHOLE = slice(0, N)


def build_samples(table, high, low, rows=WHOLE, lanes=WHOLE):
    build(table, high, low, rows, lanes)


def build_freqs(table, high, low, rows=WHOLE, lanes=WHOLE):
    build(table, high, low, rows, lanes, math.sqrt(1.0 / N))


def start(source, target, sem):
    copy = pltpu.make_async_copy(source, target, sem)
    copy.start()
    return copy


def dot(a, b):
    return jnp.dot(a, b, preferred_element_type=F32)


def stacked_times(stack, rows, high, low, columns):
    both = dot(stack[0 : 2 * rows, :], high[:, columns])
    return both[:rows] + both[rows:] + dot(stack[0:rows, :], low[:, columns])


def matrix_times(high, low, rows, pair, width, offset=0):
    both = dot(high[rows, :], pair[:, offset : offset + 2 * width])
    return both[:, :width] + both[:, width:] + dot(low[rows, :], pair[:, offset : offset + width])


def first_kernel(
    observed, estimate, spectrum, sent,
    table_v, observed_v, estimate_v, spectrum_v, sent_v, high, low, stack, sems,
):
    copies = [
        start(observed.at[0], observed_v, sems.at[1]),
        start(estimate.at[0], estimate_v, sems.at[2]),
        start(spectrum.at[0], spectrum_v, sems.at[3]),
    ]
    fill_table(table_v, True)
    copies[0].wait()
    stack[0:R, :], stack[2 * R : 3 * R, :] = split(observed_v[...])
    copies[1].wait()
    stack[R : 2 * R, :], stack[3 * R : 4 * R, :] = split(estimate_v[...])
    copies[2].wait()
    out_copies = []
    for d in range(G // 2):
        columns = slice(256 * d, 256 * d + 256)
        build_samples(table_v, high, low, WHOLE, columns)
        out = stacked_times(stack, 2 * R, high, low, columns)
        for h in range(2):
            lanes = slice(128 * h, 128 * h + 128)
            e = 2 * d + h
            sent_v[e, 0] = out[:R, lanes]
            sent_v[e, 1] = out[R:, lanes]
            sent_v[e, 2] = spectrum_v[:, 128 * e : 128 * e + 128]
        out_copies.append(
            start(sent_v.at[2 * d : 2 * d + 2], sent.at[2 * d : 2 * d + 2], sems.at[4 + d])
        )
    for copy in out_copies:
        copy.wait()


def left(x):
    return pltpu.roll(x, N - 1, 1)


def weight_of(plane, row, value, last):
    column = jnp.where(last, 0.0, left(value) - value)
    square = plane * plane + row * row + column * column
    return 1.0 / jnp.maximum(jnp.sqrt(square), HUBER_EDGE)


def divergence(value, ahead_plane, behind_plane, ahead_row, behind_row, w_plane, w_back, w_row, w_row_back, w_col):
    flux_col = w_col * (left(value) - value)
    total = w_back * (value - behind_plane) - w_plane * (ahead_plane - value)
    total += w_row_back * (value - behind_row) - w_row * (ahead_row - value)
    total += pltpu.roll(flux_col, 1, 1) - flux_col
    return SMOOTHING * total


def as_tile(row):
    return jnp.concatenate([row[:, 128 * i : 128 * i + 128] for i in range(8)], axis=0)


def weights_kernel(
    place, estimate, behind, ahead,
    sent, reg, w_all, w_back_all, strip,
    table_v, ext, ext_back, sent_v, ext_w,
    high, low, stack, sems,
):
    fill_table(table_v, True)
    ok_plane = jnp.where(place[0] < 15, 1.0, 0.0)
    ok_back = jnp.where(place[0] > 0, 1.0, 0.0)
    ext[8 : 8 + R, :] = estimate[0]
    ext_back[0:R, :] = behind[0]
    ext[7:8, :] = estimate[0, 0:1, :]
    ext[8 + R : 9 + R, :] = estimate[0, R - 1 : R, :]
    ext_back[R : R + 1, :] = behind[0, R - 1 : R, :]
    ext_w[7:8, :] = jnp.zeros((1, N), F32)
    last = lax.broadcasted_iota(jnp.int32, (CHUNK, N), 1) == N - 1
    for c in range(0, R, CHUNK):
        value = ext[8 + c : 8 + c + CHUNK, :]
        back = ext_back[c : c + CHUNK, :]
        w = weight_of(
            (ahead[0, c : c + CHUNK, :] - value) * ok_plane,
            ext[9 + c : 9 + c + CHUNK, :] - value,
            value,
            last,
        )
        ext_w[8 + c : 8 + c + CHUNK, :] = w
        w_all[c : c + CHUNK, :] = w
        w_back_all[c : c + CHUNK, :] = weight_of(
            (value - back) * ok_back, ext_back[1 + c : 1 + c + CHUNK, :] - back, back, last
        ) * ok_back
    for c in range(0, R, CHUNK):
        w = ext_w[8 + c : 8 + c + CHUNK, :]
        out = divergence(
            ext[8 + c : 8 + c + CHUNK, :],
            ahead[0, c : c + CHUNK, :],
            ext_back[c : c + CHUNK, :],
            ext[9 + c : 9 + c + CHUNK, :],
            ext[7 + c : 7 + c + CHUNK, :],
            w * ok_plane,
            w_back_all[c : c + CHUNK, :],
            w,
            ext_w[7 + c : 7 + c + CHUNK, :],
            jnp.where(last, 0.0, w),
        )
        reg[c : c + CHUNK, :] = out
        stack[c : c + CHUNK, :], stack[R + c : R + c + CHUNK, :] = split(out)
    for i, rows in enumerate((
        estimate[0, 0:2, :], estimate[0, R - 2 : R, :], ahead[0, 0:1, :], ahead[0, R - 1 : R, :],
        behind[0, 0:1, :], behind[0, R - 1 : R, :], w_all[0:1, :], w_all[R - 2 : R - 1, :],
        w_back_all[0:1, :],
    )):
        at = 2 * i if i < 2 else i + 2
        strip[at : at + rows.shape[0], :] = rows
    out_copies = []
    for d in range(G // 2):
        columns = slice(256 * d, 256 * d + 256)
        build_samples(table_v, high, low, WHOLE, columns)
        out = stacked_times(stack, R, high, low, columns)
        for h in range(2):
            e = 2 * d + h
            sent_v[e] = out[:, 128 * h : 128 * h + 128]
        out_copies.append(
            start(sent_v.at[2 * d : 2 * d + 2], sent.at[2 * d : 2 * d + 2, REG:], sems.at[1 + d])
        )
    for copy in out_copies:
        copy.wait()


def fill_edges(place, from_above, from_below, strip, sent, w_edge, stack, tiles_v, sem):
    plane, row = place[0], place[1]
    ok_plane = jnp.where(plane < 15, 1.0, 0.0)
    ok_back = jnp.where(plane > 0, 1.0, 0.0)
    ok_top = jnp.where(row > 0, 1.0, 0.0)
    inside = row < G - 1
    last = lax.broadcasted_iota(jnp.int32, (1, N), 1) == N - 1

    def line(i):
        return strip[i : i + 1, :]

    head, second, before, tail = line(0), line(1), line(2), line(3)
    top = from_above[0]
    bottom = jnp.where(inside, from_below[0], tail)
    behind_bottom = jnp.where(inside, from_below[1], line(7))
    w_top = ok_top * weight_of(
        (from_above[1] - top) * ok_plane, (head - top) * ok_top, top, last
    )
    w_tail = weight_of((line(5) - tail) * ok_plane, bottom - tail, tail, last)
    w_back_tail = ok_back * weight_of(
        (tail - line(7)) * ok_back, behind_bottom - line(7), line(7), last
    )
    w_edge[0:1, :], w_edge[1:2, :], w_edge[2:3, :] = w_top, w_tail, w_back_tail
    w_head = line(8)
    first_row = divergence(
        head, line(4), line(6), second, top,
        w_head * ok_plane, line(10), w_head, w_top, jnp.where(last, 0.0, w_head),
    )
    last_row = divergence(
        tail, line(5), line(7), bottom, before,
        w_tail * ok_plane, w_back_tail, w_tail, line(9), jnp.where(last, 0.0, w_tail),
    )
    w_edge[3:4, :], w_edge[4:5, :] = first_row, last_row
    head_tile, tail_tile = as_tile(first_row), as_tile(last_row)
    for e in range(G):
        tiles_v[e] = jnp.where(row == e - 1, tail_tile, jnp.where(row == e + 1, head_tile, 0.0))
    tile_copy = start(tiles_v, sent.at[:, EDGE:REG], sem)
    pair = jnp.concatenate([first_row, last_row, jnp.zeros((14, N), F32)], axis=0)
    stack[0:16, :], stack[16:32, :] = split(pair)
    return tile_copy


def middle_kernel(
    place, got, from_above, from_below, strip, half_sent, sent, spectral, w_edge,
    freq_v, sample_v, sent_v, f_high, f_low, s_high, s_low, pair, stack, rows_v, tiles_v, sems,
):
    tile_copy = fill_edges(
        place, from_above, from_below, strip, sent, w_edge, stack, tiles_v, sems.at[8]
    )
    fill_table(freq_v, False)
    fill_table(sample_v, True)
    for d in range(G):
        rows = slice(R * d, R * d + R)
        pair[rows, 0:128], pair[rows, 256:384] = split(got[d, 0])
        pair[rows, 128:256], pair[rows, 384:512] = split(got[d, 1])
        sent_v[d, R:] = jnp.zeros((8, 128), F32)
    for m in range(4):
        rows = slice(256 * m, 256 * m + 256)
        build_freqs(freq_v, f_high, f_low, rows)
        out = matrix_times(f_high, f_low, rows, pair, 256)
        gain = jnp.concatenate([got[2 * m, 2], got[2 * m + 1, 2]], axis=0)
        value = gain * (out[:, :128] - gain * out[:, 128:])
        spectral[rows, :128] = value
        spectral[rows, 128:] = gain
        pair[rows, 512:640], pair[rows, 640:768] = split(value)
    out_copies = []
    for m in range(4):
        rows = slice(256 * m, 256 * m + 256)
        build_samples(sample_v, s_high, s_low, rows)
        out = matrix_times(s_high, s_low, rows, pair, 128, 512)
        for h in range(2):
            d = 2 * m + h
            block = out[R * h : R * h + R]
            sent_v[d, 0:R] = block
            if d + 1 < G:
                sent_v[d + 1, R : R + 1] = block[R - 1 : R]
            if d > 0:
                sent_v[d - 1, R + 1 : R + 2] = block[0:1]
                out_copies.append(start(sent_v.at[d - 1], sent.at[d - 1, 0:EDGE], sems.at[d]))
    out_copies.append(start(sent_v.at[G - 1], sent.at[G - 1, 0:EDGE], sems.at[0]))
    for d in range(G // 2):
        out = stacked_times(stack, 16, s_high, s_low, slice(256 * d, 256 * d + 256))
        for h in range(2):
            e = 2 * d + h
            rows_v[e] = out[0:8, 128 * h : 128 * h + 128]
            for i, at in enumerate((0, R - 1)):
                out_copies.append(
                    start(rows_v.at[e, i : i + 1], sent.at[e, REG + at : REG + at + 1], sems.at[9 + 2 * e + i])
                )
    tile_copy.wait()
    for copy in out_copies:
        copy.wait()


def residual_kernel(
    place, got, reg, w_edge, residual, edges, table_v, rows_v, f_high, f_low, stack,
):
    row = place[1]
    fill_table(table_v, False)
    above = got[jnp.maximum(row - 1, 0), EDGE:REG, :]
    below = got[jnp.minimum(row + 1, G - 1), EDGE:REG, :]
    for i in range(G):
        rows_v[0:1, 128 * i : 128 * i + 128] = above[i : i + 1]
        rows_v[1:2, 128 * i : 128 * i + 128] = below[i : i + 1]
    rows = R + 16
    for d in range(G):
        lanes = slice(128 * d, 128 * d + 128)
        stack[0:rows, lanes], stack[rows : 2 * rows, lanes] = split(got[d, 0:rows])
    for d in range(G // 2):
        lanes = slice(256 * d, 256 * d + 256)
        build_freqs(table_v, f_high, f_low, WHOLE, lanes)
        out = stacked_times(stack, rows, f_high, f_low, lanes)
        residual[0, :, lanes] = out[:R] - reg[:, lanes]
        residual[0, 0:1, lanes] = out[0:1] - w_edge[3:4, lanes]
        residual[0, R - 1 : R, lanes] = out[R - 1 : R] - w_edge[4:5, lanes]
        edges[0:2, lanes] = out[R : R + 2] - rows_v[0:2, lanes]


def curvature_kernel(
    got, spectral, sent, total, freq_v, sample_v, sent_v, f_high, f_low, s_high, s_low, pair, sems,
):
    fill_table(freq_v, False)
    fill_table(sample_v, True)
    for d in range(G):
        rows = slice(R * d, R * d + R)
        pair[rows, 0:128], pair[rows, 128:256] = split(got[d, REG:])
    acc = jnp.zeros((8, 128), F32)
    for m in range(4):
        rows = slice(256 * m, 256 * m + 256)
        build_freqs(freq_v, f_high, f_low, rows)
        out = spectral[rows, :128] - matrix_times(f_high, f_low, rows, pair, 128)
        gain = spectral[rows, 128:]
        scaled = gain * gain * out
        acc += jnp.sum((scaled * out).reshape(32, 8, 128), axis=0)
        pair[rows, 256:384], pair[rows, 384:512] = split(scaled)
    total[...] = acc
    out_copies = []
    for m in range(4):
        rows = slice(256 * m, 256 * m + 256)
        build_samples(sample_v, s_high, s_low, rows)
        out = matrix_times(s_high, s_low, rows, pair, 128, 256)
        sent_v[2 * m] = out[:R]
        sent_v[2 * m + 1] = out[R:]
        out_copies.append(
            start(sent_v.at[2 * m : 2 * m + 2], sent.at[2 * m : 2 * m + 2, 0:R], sems.at[m])
        )
    for copy in out_copies:
        copy.wait()


def patched(weights, w_edge, c, line):
    w = weights[c : c + CHUNK, :]
    if c + CHUNK < R:
        return w
    row = lax.broadcasted_iota(jnp.int32, (CHUNK, N), 0)
    return jnp.where(row == CHUNK - 1, w_edge[line : line + 1, :], w)


def extend(place, residual, edges, ext):
    ext[7:8, :] = edges[0:1, :]
    ext[8 : 8 + R, :] = residual[0]
    ext[8 + R : 9 + R, :] = jnp.where(place[1] < G - 1, edges[1:2, :], residual[0, R - 1 : R, :])


def partial_kernel(place, residual, edges, w_all, w_edge, parts, ext):
    extend(place, residual, edges, ext)
    last = lax.broadcasted_iota(jnp.int32, (CHUNK, N), 1) == N - 1
    norm = jnp.zeros((8, N), F32)
    product = jnp.zeros((8, N), F32)
    for c in range(0, R, CHUNK):
        value = ext[8 + c : 8 + c + CHUNK, :]
        row = ext[9 + c : 9 + c + CHUNK, :] - value
        column = jnp.where(last, 0.0, left(value) - value)
        cross = (SMOOTHING * patched(w_all, w_edge, c, 1)) * (row * row + column * column)
        square = value * value
        norm += square[:8] + square[8:]
        product += cross[:8] + cross[8:]
    parts[0] = norm
    parts[1] = product


def product_kernel(
    place, residual, ahead, w_all, w_edge, parts, total, half, sent, tile_v, sems,
):
    acc = jnp.zeros((8, N), F32)
    for c in range(0, R, CHUNK):
        plane = ahead[0, c : c + CHUNK, :] - residual[0, c : c + CHUNK, :]
        cross = patched(w_all, w_edge, c, 1) * (plane * plane)
        acc += cross[:8] + cross[8:]
    product = parts[1] + jnp.where(place[0] < 15, SMOOTHING, 0.0) * acc
    norm = jnp.sum(as_tile(jnp.sum(parts[0], axis=0, keepdims=True)), axis=0, keepdims=True)
    product = as_tile(jnp.sum(product, axis=0, keepdims=True)) + total[...]
    product = jnp.sum(product, axis=0, keepdims=True)
    tile_v[...] = jnp.concatenate([norm, product, jnp.zeros((6, 128), F32)], axis=0)
    out_copies = [start(tile_v, sent.at[d, R:], sems.at[d]) for d in range(G)]
    for copy in out_copies:
        copy.wait()


def inner_kernel(
    place, residual, behind, ahead, edges, w_all, w_back_all, w_edge, image, ext, ext_w,
):
    ok_plane = jnp.where(place[0] < 15, 1.0, 0.0)
    extend(place, residual, edges, ext)
    ext_w[7:8, :] = w_edge[0:1, :]
    ext_w[8 : 8 + R, :] = w_all[...]
    ext_w[7 + R : 8 + R, :] = w_edge[1:2, :]
    last = lax.broadcasted_iota(jnp.int32, (CHUNK, N), 1) == N - 1
    for c in range(0, R, CHUNK):
        w = ext_w[8 + c : 8 + c + CHUNK, :]
        image[c : c + CHUNK, :] = divergence(
            ext[8 + c : 8 + c + CHUNK, :],
            ahead[0, c : c + CHUNK, :],
            behind[0, c : c + CHUNK, :],
            ext[9 + c : 9 + c + CHUNK, :],
            ext[7 + c : 7 + c + CHUNK, :],
            w * ok_plane,
            patched(w_back_all, w_edge, c, 2),
            w,
            ext_w[7 + c : 7 + c + CHUNK, :],
            jnp.where(last, 0.0, w),
        )


def last_kernel(
    sums, got, reg, residual, estimate, restored, final,
    table_v, restored_v, final_v, f_high, f_low, stack, sems,
):
    fill_table(table_v, False)
    for d in range(G):
        lanes = slice(128 * d, 128 * d + 128)
        stack[0:R, lanes], stack[R : 2 * R, lanes] = split(got[d, 0:R])
    tile = jnp.sum(sums[...], axis=0)
    norm = jnp.sum(tile[0:1, :], axis=1, keepdims=True)
    product = jnp.sum(tile[1:2, :], axis=1, keepdims=True)
    step = norm / product
    restored_v[...] = estimate[0] + step * residual[0]
    out_copies = [start(restored_v, restored.at[0], sems.at[4])]
    for d in range(G // 2):
        lanes = slice(256 * d, 256 * d + 256)
        build_freqs(table_v, f_high, f_low, WHOLE, lanes)
        image = stacked_times(stack, R, f_high, f_low, lanes) + reg[:, lanes]
        final_v[:, lanes] = residual[0, :, lanes] - step * image
        out_copies.append(start(final_v.at[:, lanes], final.at[0, :, lanes], sems.at[d]))
    for copy in out_copies:
        copy.wait()


def across(x, axes):
    return lax.all_to_all(x, axes, split_axis=0, concat_axis=0, tiled=True)


def field(rows=R):
    return pltpu.VMEM((rows, N), F32)


def step(observed, estimate, spectrum):
    planes, groups = 16, G
    place = jnp.stack([lax.axis_index(PLANES), lax.axis_index(ROWS)]).astype(jnp.int32)
    up = [(i, i + 1) for i in range(planes - 1)]
    down = [(i + 1, i) for i in range(planes - 1)]
    row_up = [(i, i + 1) for i in range(groups - 1)]
    row_down = [(i + 1, i) for i in range(groups - 1)]
    big = 2 * N * N * R
    block = shape(R, N)

    behind = lax.ppermute(estimate, PLANES, up)
    ahead = lax.ppermute(estimate, PLANES, down)
    sent = call(
        first_kernel,
        (shape(G, 3, R, 128),),
        6 * big,
        (TABLE, field(), field(), field(), pltpu.VMEM((G, 3, R, 128), F32), MATRIX, MATRIX,
         pltpu.VMEM((4 * R, N), BF16), DMA((8,))),
        (ANY,), limit=60,
    )(observed, estimate, spectrum)[0]
    first = across(sent, ROWS)

    tails = jnp.concatenate([estimate[:, R - 1 :], ahead[:, R - 1 :]], axis=0)
    heads = jnp.concatenate([estimate[:, :1], behind[:, :1]], axis=0)
    from_above = lax.ppermute(tails, ROWS, row_up)
    from_below = lax.ppermute(heads, ROWS, row_down)
    wide = shape(G, FULL, 128)
    half_sent, reg, w_all, w_back, strip = call(
        weights_kernel,
        (wide, block, block, block, shape(16, N)),
        3 * big,
        (TABLE, field(R + 16), field(R + 8), pltpu.VMEM((G, R, 128), F32),
         field(R + 16), MATRIX, MATRIX, pltpu.VMEM((2 * R, N), BF16), DMA((5,))),
        (ANY, VMEM, VMEM, VMEM, VMEM), direct=4,
    )(place, estimate, behind, ahead)
    sent, spectral, w_edge = call(
        middle_kernel,
        (wide, shape(N, 256), shape(8, N)),
        9 * big,
        (TABLE, TABLE, pltpu.VMEM((G, EDGE, 128), F32), MATRIX, MATRIX, MATRIX, MATRIX,
         pltpu.VMEM((N, 768), BF16), pltpu.VMEM((32, N), BF16), pltpu.VMEM((G, 8, 128), F32),
         pltpu.VMEM((G, 8, 128), F32), DMA((25,))),
        (ANY, VMEM, VMEM), {5: 0}, direct=5,
    )(place, first, from_above, from_below, strip, half_sent)
    second = across(sent, ROWS)

    residual, edges = call(
        residual_kernel,
        (shape(1, R, N), shape(8, N)),
        3 * big,
        (TABLE, field(8), MATRIX, MATRIX, pltpu.VMEM((2 * R + 32, N), BF16)),
        direct=9,
    )(place, second, reg, w_edge)
    ahead = lax.ppermute(residual, PLANES, down)
    parts = call(
        partial_kernel, (shape(2, 8, N),), big // 16, (field(R + 16),), direct=9
    )(place, residual, edges, w_all, w_edge)[0]
    half_sent, total = call(
        curvature_kernel,
        (shape(G, EDGE, 128), shape(8, 128)),
        6 * big,
        (TABLE, TABLE, pltpu.VMEM((G, R, 128), F32), MATRIX, MATRIX, MATRIX, MATRIX,
         pltpu.VMEM((N, 512), BF16), DMA((4,))),
        (ANY, VMEM), direct=2,
    )(second, spectral)
    late, _ = lax.optimization_barrier((residual, ahead))
    behind = lax.ppermute(late, PLANES, up)
    sent = call(
        product_kernel,
        (shape(G, EDGE, 128),),
        big // 64,
        (pltpu.VMEM((8, 128), F32), DMA((8,))),
        (ANY,), {7: 0}, direct=7,
    )(place, residual, ahead, w_all, w_edge, parts, total, half_sent)[0]
    third = across(sent, ROWS)
    reg_residual = call(
        inner_kernel, (block,), big // 16, (field(R + 16), field(R + 16)), direct=9
    )(place, residual, behind, ahead, edges, w_all, w_back, w_edge)[0]
    tile = jnp.sum(third[:, R:], axis=0)
    sums = across(jnp.broadcast_to(tile[None], (planes, 8, 128)), PLANES)
    return call(
        last_kernel,
        (shape(1, R, N), shape(1, R, N)),
        3 * big,
        (TABLE, field(), field(), MATRIX, MATRIX, pltpu.VMEM((2 * R, N), BF16), DMA((5,))),
        (ANY, ANY), direct=9,
    )(sums, third, reg_residual, residual, estimate)


def solution(mesh):
    finer = Mesh(
        mesh.devices.reshape(4, 2, 2, 2, 4),
        ("planes_0", "planes_1", "planes_2", "rows_0", "rows_1"),
    )
    spec = P(PLANES, ROWS, None)
    return jax.shard_map(
        step,
        mesh=finer,
        in_specs=(spec, spec, spec),
        out_specs=(spec, spec),
        check_vma=False,
    )
```
